256 devices in a mesh: trade: 8 (over z), path: 32 (over x, y, core).
Axes of the slice: x: 4, y: 4, z: 8, core: 2. Of those that a mesh axis runs over, the one named last changes fastest.
Arguments:
- start_state: float32 [16384, 32], P('path'), may hold values from -6 to 6
- shocks: float32 [2, 16384, 32], P(None, 'path'), may hold values from -6 to 6
- loadings: float32 [32, 65536], P(None, 'trade'), may hold values from -1 to 1
- strikes: float32 [65536], P('trade'), may hold values from -0.5 to 1
- notionals: float32 [65536], P('trade'), may hold values from -1 to 1
- trade_set: int32 [65536], P('trade'), may hold values from 0 to 2047
- live_counts: int32 [8], replicated, may hold values from 1 to 8192, 49152 in all
- weights: int32 [16384], P('path'), may hold values from 1 to 16
- thresholds: int32 [2048], P('trade'), may hold values from 0 to 8
Outputs:
- exposure: float32 [2, 2048, 16384], P(None, 'trade', 'path')
- expected: float32 [2, 2048], P(None, 'trade')
The draws below stay inside these ranges and needn't reach their ends.
Inputs may be any that keep to these rules, and one draw needn't show every extreme that they name: The live slots of group g are its first live_counts[g] slots; the counts sum to 49152 and some group is full.
All inputs are finite; a program needn't handle non-finite values.
Results may differ from the reference program's by a relative error of at most 0.0003.
Values sent between devices are 32-bit elements; how exact they have to be, the bound alone decides.
A program may use at most 128 MiB of HBM per device.

```python
import math
import jax
import jax.numpy as jnp
import numpy as np
from jax import lax

NF = 32
DATES = 2
TR_DEV = 8192
GROUPS = 8
PATHS = 16384
TRADES = 65536
NSETS = 2048
LIVE = 49152


def place_ends(array, stream_key, low, top_value):
    spot = [jax.random.randint(jax.random.fold_in(stream_key, axis), (), 0, length) for axis, length in enumerate(array.shape)]
    longest = array.shape.index(max(array.shape))
    neighbour = spot[:longest] + [(spot[longest] + 1) % array.shape[longest]] + spot[longest + 1:]
    return array.at[tuple(spot)].set(low).at[tuple(neighbour)].set(top_value)


def level_of(rng, dims, split, low, top_value):
    def one(dim, shards_of):
        draws = jax.random.uniform(jax.random.fold_in(jax.random.fold_in(rng, 6), dim), (shards_of,), jnp.float32, low / len(split), top_value / len(split))
        return jnp.repeat(jnp.exp(draws), dims[dim] // shards_of).reshape((-1,) + (1,) * (len(dims) - dim - 1))

    level = one(*split[0])
    for cut in split[1:]:
        level = level * one(*cut)
    return level


def split_up(amount, total, limit, lean):
    loads = [(1 << 20) // math.isqrt(standing ** lean) + 1 for standing in range(2, amount + 1)]
    rest, given = total - limit - (amount - 1), [1] * (amount - 1)
    while rest > 0:
        movable = [i for i in range(amount - 1) if given[i] < limit]
        pool, remaining = sum([loads[i] for i in movable]), rest
        for i in movable:
            extra = min(limit - given[i], max(1, remaining * loads[i] // pool), rest)
            given[i] = given[i] + extra
            rest = rest - extra
    return np.array([limit] + given)


def uneven(stream_key, number_of, total, bound, slope):
    if number_of == 2:
        one = jax.random.randint(stream_key, (), max(1, total - bound), min(bound, total - 1) + 1)
        return jnp.stack([one, total - one])
    sizes = jnp.asarray(split_up(number_of, total, bound, slope), jnp.int32)
    couples = (number_of - 1) // 2
    donor, taker = sizes[1:1 + 2 * couples:2], sizes[2:2 + 2 * couples:2]
    slack = jnp.minimum(donor - 1, bound - taker)
    shifted = jax.random.randint(jax.random.fold_in(stream_key, 1), (couples,), 0, 1 << 20) % (slack + 1)
    sizes = sizes.at[1:1 + 2 * couples:2].set(donor - shifted).at[2:2 + 2 * couples:2].set(taker + shifted)
    return sizes[jax.random.permutation(jax.random.fold_in(stream_key, 2), number_of)]


def normal_values(stream_key, dims, width, most, shards=(), kind=jnp.bfloat16):
    entries = jax.random.normal(stream_key, dims, jnp.float32) * width
    if len(shards) > 0:
        entries = level_of(stream_key, dims, shards, -0.22, 0.18) * entries
    return jnp.clip(entries, min=-most, max=most).astype(kind)


def setup_inputs(seed: int = 0) -> dict:
    keys = jax.random.split(jax.random.key(seed), 10)
    return {
        "start_state": normal_values(keys[0], (PATHS, NF), 1.0, 6.0, ((0, 32),), jnp.float32),
        "shocks": normal_values(keys[1], (DATES, PATHS, NF), 1.0, 6.0, ((1, 32),), jnp.float32),
        "loadings": normal_values(keys[2], (NF, TRADES), NF ** -0.5, 1.0, ((1, 8),), jnp.float32),
        "strikes": jnp.clip(-0.5 + 1.5 * jax.random.uniform(keys[3], (TRADES,), jnp.float32) ** level_of(keys[3], (TRADES,), ((0, 8),), -0.2, 0.2), -0.5, 1.0),
        "notionals": jnp.clip(jax.random.uniform(keys[4], (TRADES,), jnp.float32, -1.0, 1.0) * level_of(keys[4], (TRADES,), ((0, 8),), -0.4, 0.0), -1.0, 1.0),
        "trade_set": place_ends(jax.random.randint(keys[5], (TRADES,), 0, NSETS), jax.random.fold_in(keys[5], 1), 0, NSETS - 1).astype(jnp.int32),
        "live_counts": uneven(keys[6], GROUPS, LIVE, TR_DEV, 2).astype(jnp.int32),
        "weights": place_ends(jax.random.randint(keys[7], (PATHS,), 1, 17), jax.random.fold_in(keys[7], 1), 1, 16).astype(jnp.int32),
        "thresholds": place_ends(jax.random.randint(keys[8], (NSETS,), 0, 9), jax.random.fold_in(keys[8], 1), 0, 8).astype(jnp.int32),
    }


HIGHEST_PREC = lax.Precision.HIGHEST
ROOT_HALF = 0.7071067811865476

def make_basis(state):
    return jnp.concatenate([state, (state * state - 1.0) * ROOT_HALF], axis=1)

def reference(start_state, shocks, loadings, strikes, notionals, trade_set, live_counts, weights, thresholds):
    weight_vals = weights.astype(jnp.float32)
    states = [start_state]
    for date_idx in range(DATES):
        states.append(0.8 * states[-1] + 0.6 * shocks[date_idx])
    slots = jnp.arange(TRADES, dtype=jnp.int32)
    owners = slots // TR_DEV
    live = (slots % TR_DEV < live_counts[owners]).astype(jnp.float32)
    scaled = notionals * live
    limits = 0.25 * thresholds.astype(jnp.float32)
    exposures = []
    expects = []
    for date_idx in range(DATES):
        basis_vals = make_basis(states[date_idx])
        weighted = basis_vals * weight_vals[:, None]
        gram_total = jnp.dot(weighted.T, basis_vals, precision=HIGHEST_PREC)
        future = states[date_idx + 1]

        def block_step(netted, block_idx):
            begin = (block_idx * TR_DEV).astype(jnp.int32)
            load_block = lax.dynamic_slice_in_dim(loadings, begin, TR_DEV, 1)
            strike_block = lax.dynamic_slice_in_dim(strikes, begin, TR_DEV, 0)
            scale_block = lax.dynamic_slice_in_dim(scaled, begin, TR_DEV, 0)
            set_block = lax.dynamic_slice_in_dim(trade_set, begin, TR_DEV, 0)
            cashflow = scale_block * jnp.maximum(jnp.dot(future, load_block, precision=HIGHEST_PREC) - strike_block, 0.0)
            moment = jnp.dot(weighted.T, cashflow, precision=HIGHEST_PREC)
            coeffs = jnp.linalg.solve(gram_total, moment)
            values = jnp.dot(coeffs.T, basis_vals.T, precision=HIGHEST_PREC)
            netted = netted + jax.ops.segment_sum(values, set_block, num_segments=NSETS)
            return (netted, None)
        netted, _ = lax.scan(block_step, jnp.zeros((NSETS, PATHS), jnp.float32), jnp.arange(GROUPS, dtype=jnp.int32))
        clamped = jnp.maximum(netted - limits[:, None], 0.0)
        exposures.append(clamped)
        expects.append(jnp.dot(clamped, weight_vals, precision=HIGHEST_PREC) / jnp.sum(weight_vals))
    return (jnp.stack(exposures), jnp.stack(expects))
```

```python
import functools

import jax
import jax.numpy as jnp
from jax import lax
from jax.experimental import pallas as pl
from jax.experimental.pallas import tpu as pltpu
from jax.sharding import PartitionSpec as P

ROOT_HALF = 0.7071067811865476
F32, BF16 = jnp.float32, jnp.bfloat16
HIGHEST = lax.Precision.HIGHEST
MESH = pl.DeviceIdType.MESH
LANES = 128


def split(value):
    high = value.astype(BF16)
    return high, (value - high.astype(F32)).astype(BF16)


def dot(left, right, left_dim, right_dim, precision=None):
    return lax.dot_general(
        left, right, (((left_dim,), (right_dim,)), ((), ())), precision=precision, preferred_element_type=F32
    )


def prepare(start_ref, shocks_ref, weights_ref, state_ref, wbasis_ref, basis_ref, gram_ref):
    paths, factors = start_ref.shape
    width = 2 * factors
    dates = shocks_ref.shape[0]
    weight = weights_ref[...].astype(F32)
    state = start_ref[...].T
    wbasis_ref[...] = jnp.zeros_like(wbasis_ref)
    grams = []
    for date in range(dates):
        future = 0.8 * state + 0.6 * shocks_ref[date].T
        cols = pl.ds(date * paths, paths)
        high, low = split(future)
        state_ref[0:factors, cols] = high
        state_ref[factors : 2 * factors, cols] = high
        state_ref[2 * factors : 3 * factors, cols] = low
        row = lax.broadcasted_iota(jnp.int32, (factors, paths), 0)
        state_ref[3 * factors : 4 * factors, cols] = jnp.where(row < 3, 1.0, 0.0).astype(BF16)
        basis = jnp.concatenate([state, (state * state - 1.0) * ROOT_HALF], axis=0)
        basis_ref[date] = basis
        weighted = basis * weight
        high, low = split(weighted)
        wbasis_ref[date * width : (date + 1) * width, cols] = high
        wbasis_ref[dates * width + date * width : dates * width + (date + 1) * width, cols] = low
        grams.append(dot(weighted, basis, 1, 1, HIGHEST))
        state = future
    gram_ref[0:width, :] = jnp.concatenate(grams, axis=1)
    gram_ref[width : width + 8, :] = jnp.broadcast_to(jnp.sum(weight, axis=1, keepdims=True), (8, LANES))


def scaled_trades(loadings_ref, strikes_ref, notionals_ref, block, size):
    cols = pl.ds(pl.multiple_of(block * size, size), size)
    scale = jnp.abs(notionals_ref[:, cols])
    high, low = split(loadings_ref[:, cols] * scale)
    strike = strikes_ref[:, cols] * (-scale)
    first = strike.astype(BF16).astype(F32)
    second = (strike - first).astype(BF16).astype(F32)
    third = (strike - first) - second
    row = lax.broadcasted_iota(jnp.int32, high.shape, 0)
    parts = jnp.where(row == 0, first, jnp.where(row == 1, second, jnp.where(row == 2, third, 0.0)))
    return jnp.concatenate([high, low, high, parts.astype(BF16)], axis=0)


def moments_of(values, wbasis_ref, moment_ref, block, size):
    high, low = split(jnp.maximum(values, 0.0))
    both = dot(high, wbasis_ref[...], 1, 1)
    more = dot(low, wbasis_ref[0:LANES, :], 1, 1)
    moment = both[:, :LANES] + both[:, LANES:] + more
    high, low = split(moment)
    rows = pl.ds(pl.multiple_of(block * size, size), size)
    moment_ref[rows, 0:LANES] = high
    moment_ref[rows, LANES : 2 * LANES] = low


def local_kernel(
    size, set_size, start_ref, shocks_ref, loadings_ref, strikes_ref, notionals_ref, sets_ref, filled_ref, weights_ref,
    netted_ref, gram_ref, basis_ref, state_ref, wbasis_ref, moment_ref, values_ref, index_ref, sign_ref,
):
    slots = loadings_ref.shape[1]
    blocks = slots // size
    prepare(start_ref, shocks_ref, weights_ref, state_ref, wbasis_ref, basis_ref, gram_ref)

    def flows(block):
        return dot(scaled_trades(loadings_ref, strikes_ref, notionals_ref, block, size), state_ref[...], 0, 0)

    values_ref[0] = flows(0)

    def step(block, carry):
        values = values_ref[lax.rem(block, 2)]
        values_ref[lax.rem(block + 1, 2)] = flows(jnp.minimum(block + 1, blocks - 1))
        moments_of(values, wbasis_ref, moment_ref, block, size)
        return carry

    lax.fori_loop(0, blocks, step, 0)

    slot = lax.broadcasted_iota(jnp.int32, (1, slots), 1)
    index_ref[...] = jnp.where(slot < filled_ref[0], sets_ref[...], -1)
    notional = notionals_ref[...]
    sign_ref[...] = jnp.where(notional > 0, 1.0, jnp.where(notional < 0, -1.0, 0.0))

    def net(chunk, carry):
        row = lax.broadcasted_iota(jnp.int32, (set_size, slots), 0) + chunk * set_size
        member = jnp.where(row == index_ref[...], sign_ref[...], 0.0).astype(BF16)
        both = dot(member, moment_ref[...], 1, 0)
        rows = pl.ds(pl.multiple_of(chunk * set_size, set_size), set_size)
        netted_ref[rows, :] = both[:, :LANES] + both[:, LANES:]
        return carry

    lax.fori_loop(0, netted_ref.shape[0] // set_size, net, 0)


def local_moments(start, shocks, loadings, strikes, notionals, sets, filled, weights, set_count):
    paths, factors = start.shape
    dates = shocks.shape[0]
    slots = loadings.shape[1]
    size, set_size = min(1024, slots), min(512, set_count)
    vmem = pl.BlockSpec(memory_space=pltpu.VMEM)
    return pl.pallas_call(
        functools.partial(local_kernel, size, set_size),
        out_shape=(
            jax.ShapeDtypeStruct((set_count, LANES), F32),
            jax.ShapeDtypeStruct((2 * factors + 8, LANES), F32),
            jax.ShapeDtypeStruct((dates, 2 * factors, paths), F32),
        ),
        in_specs=[vmem] * 6 + [pl.BlockSpec(memory_space=pltpu.SMEM), vmem],
        out_specs=(vmem, vmem, vmem),
        scratch_shapes=[
            pltpu.VMEM((4 * factors, dates * paths), BF16),
            pltpu.VMEM((2 * LANES, dates * paths), BF16),
            pltpu.VMEM((slots, 2 * LANES), BF16),
            pltpu.VMEM((2, size, dates * paths), F32),
            pltpu.VMEM((1, slots), jnp.int32),
            pltpu.VMEM((1, slots), F32),
        ],
        compiler_params=pltpu.CompilerParams(vmem_limit_bytes=56 << 20),
        name="local_moments",
    )(
        start, shocks, loadings, strikes.reshape(1, -1), notionals.reshape(1, -1), sets.reshape(1, -1),
        filled.reshape(1), weights.reshape(1, -1),
    )


def invert(matrix_ref):
    size = matrix_ref.shape[0]
    lane = lax.broadcasted_iota(jnp.int32, (size, LANES), 1)
    row_id = lax.broadcasted_iota(jnp.int32, (size, LANES), 0)
    left = lane < size
    lane_row = lax.broadcasted_iota(jnp.int32, (1, LANES), 1)

    def step(j, carry):
        matrix = matrix_ref[...]
        row = matrix_ref[pl.ds(j, 1), :]

        def pick(entries, ids):
            first = jnp.sum(jnp.where(ids == j, entries, 0.0), axis=1, keepdims=True)
            second = jnp.sum(jnp.where(ids == j + size, entries, 0.0), axis=1, keepdims=True)
            return jnp.where(ids < size, first, second)

        column = pick(matrix, lane)
        inverse = 1.0 / pick(row, lane_row)
        scaled = row * inverse
        here = jnp.logical_or(lane == j, lane == j + size)
        reduced = jnp.where(here, -column * inverse, matrix - column * scaled)
        pivot_row = jnp.where(jnp.logical_or(lane_row == j, lane_row == j + size), inverse, scaled)
        matrix_ref[...] = jnp.where(row_id == j, pivot_row, reduced)
        return carry

    lax.fori_loop(0, size, step, 0)
    return left


def exchange_kernel(
    zs, xys, netted_ref, gram_ref, basis_ref, weights_ref, thresholds_ref,
    exposure_ref, expected_ref,
    gram_out, gram_in, gram_sum, gram_all, matrix_ref, core_in, plane_out, plane_in, z_out, z_in, own_ref, coeffs_ref,
    part_ref,
    gram_send, gram_recv, gall_send, gall_recv, core_send, core_recv, plane_send, plane_recv, z_send, z_recv,
    coeff_send, coeff_recv, part_send, part_recv,
):
    z = lax.axis_index("trade")
    q = lax.axis_index("path")
    xy, core = q // 2, lax.rem(q, 2)
    qs = 2 * xys
    width = basis_ref.shape[1]
    dates = basis_ref.shape[0]

    barrier = pltpu.get_barrier_semaphore()

    def greet(o, carry):
        pl.semaphore_signal(barrier, inc=1, device_id=(z, lax.rem(q + o, qs)), device_id_type=MESH)
        return carry

    lax.fori_loop(1, qs, greet, 0)

    def greet_z(o, carry):
        pl.semaphore_signal(barrier, inc=1, device_id=(lax.rem(z + o, zs), q), device_id_type=MESH)
        return carry

    lax.fori_loop(1, zs, greet_z, 0)
    pl.semaphore_wait(barrier, qs - 1 + zs - 1)

    def copy(src, dst, send, recv, device):
        return pltpu.make_async_remote_copy(
            src_ref=src, dst_ref=dst, send_sem=send, recv_sem=recv, device_id=device, device_id_type=MESH
        )

    def each(count, make, act):
        def body(o, carry):
            act(make(o))
            return carry

        lax.fori_loop(1, count, body, 0)

    other = 1 - core

    def core_copy():
        return copy(netted_ref.at[:, other], core_in, core_send, core_recv, (z, xy * 2 + other))

    core_copy().start()

    rows = width // qs

    def gram_copy(o):
        to = lax.rem(q + o, qs)
        return copy(gram_out.at[to], gram_in.at[o], gram_send.at[o], gram_recv.at[o], (z, to))

    for piece in range(qs):
        gram_out[piece, 0:rows, :] = gram_ref[piece * rows : (piece + 1) * rows, :]
        gram_out[piece, rows : rows + 1, :] = gram_ref[width : width + 1, :]
    each(qs, gram_copy, lambda c: c.start())
    gram_in[0] = gram_out[q]

    core_copy().wait()
    plane_out[...] = netted_ref[:, core] + core_in[...]

    def plane_copy(o):
        to = lax.rem(xy + o, xys)
        return copy(plane_out.at[:, to], plane_in.at[o], plane_send.at[o], plane_recv.at[o], (z, to * 2 + core))

    each(xys, plane_copy, lambda c: c.start())
    plane_in[0] = plane_out[:, xy]

    each(qs, gram_copy, lambda c: c.wait())
    gram_sum[...] = jnp.sum(gram_in[...], axis=0)

    def gall_copy(o):
        to = lax.rem(q + o, qs)
        return copy(gram_sum, gram_all.at[q], gall_send.at[o], gall_recv.at[o], (z, to))

    each(qs, gall_copy, lambda c: c.start())
    gram_all[q] = gram_sum[...]

    each(xys, plane_copy, lambda c: c.wait())
    z_out[...] = jnp.sum(plane_in[...], axis=0)

    def z_copy(o):
        to = lax.rem(z + o, zs)
        return copy(z_out.at[to], z_in.at[o], z_send.at[o], z_recv.at[o], (to, q))

    each(zs, z_copy, lambda c: c.start())
    z_in[0] = z_out[z]

    def gall_wait(o):
        return copy(gram_sum, gram_all.at[lax.rem(q + qs - o, qs)], gall_send.at[o], gall_recv.at[o], (z, q))

    each(qs, gall_copy, lambda c: c.wait_send())
    each(qs, gall_wait, lambda c: c.wait_recv())
    for piece in range(qs):
        matrix_ref[piece * rows : (piece + 1) * rows, :] = gram_all[piece, 0:rows, :]
    total = gram_all[0, rows : rows + 1, 0:1]
    left = invert(matrix_ref)
    inverse = matrix_ref[...]
    block = jnp.concatenate([jnp.where(left, inverse, 0.0), jnp.where(left, 0.0, inverse)], axis=0)

    each(zs, z_copy, lambda c: c.wait())
    moment = jnp.sum(z_in[...], axis=0)
    own_ref[...] = dot(moment, block, 1, 0, HIGHEST)

    def coeff_copy(o):
        to = lax.rem(q + o, qs)
        return copy(own_ref, coeffs_ref.at[core, xy], coeff_send.at[o], coeff_recv.at[o], (z, to))

    def coeff_wait(o):
        src = lax.rem(q + qs - o, qs)
        return copy(own_ref, coeffs_ref.at[lax.rem(src, 2), src // 2], coeff_send.at[o], coeff_recv.at[o], (z, q))

    each(qs, coeff_copy, lambda c: c.start())
    coeffs_ref[core, xy] = own_ref[...]
    weight = jnp.broadcast_to(weights_ref[...].astype(F32), (8, weights_ref.shape[1])).astype(BF16)
    sets = thresholds_ref.shape[1]
    limits = jnp.broadcast_to(0.25 * thresholds_ref[...].astype(F32), (LANES, sets)).T
    each(qs, coeff_copy, lambda c: c.wait_send())
    each(qs, coeff_wait, lambda c: c.wait_recv())

    coeffs = coeffs_ref[...].reshape(sets, LANES)
    for date in range(dates):
        netted = dot(coeffs[:, date * width : (date + 1) * width], basis_ref[date], 1, 0, HIGHEST)
        exposure = jnp.maximum(netted - limits[:, 0:1], 0.0)
        exposure_ref[date] = exposure
        high, low = split(exposure)
        part = dot(weight, high, 1, 1) + dot(weight, low, 1, 1)
        part_ref[q, date : date + 1, :] = part[0:1, :]

    def part_copy(o):
        to = lax.rem(q + o, qs)
        return copy(part_ref.at[q], part_ref.at[q], part_send.at[o], part_recv.at[o], (z, to))

    def part_wait(o):
        src = lax.rem(q + qs - o, qs)
        return copy(part_ref.at[q], part_ref.at[src], part_send.at[o], part_recv.at[o], (z, q))

    each(qs, part_copy, lambda c: c.start())
    each(qs, part_copy, lambda c: c.wait_send())
    each(qs, part_wait, lambda c: c.wait_recv())
    expected_ref[...] = jnp.sum(part_ref[...], axis=0) / total


def exchange(netted, gram, basis, weights, thresholds, zs, qs):
    xys = qs // 2
    dates, width, paths = basis.shape
    sets = thresholds.shape[0]
    per = sets // qs
    tall = (width // qs + 8) // 8 * 8
    vmem = pl.BlockSpec(memory_space=pltpu.VMEM)
    dma = pltpu.SemaphoreType.DMA
    return pl.pallas_call(
        functools.partial(exchange_kernel, zs, xys),
        out_shape=(
            jax.ShapeDtypeStruct((dates, sets, paths), F32),
            jax.ShapeDtypeStruct((dates, sets), F32),
        ),
        in_specs=[vmem] * 5,
        out_specs=(vmem, vmem),
        scratch_shapes=[
            pltpu.VMEM((qs, tall, LANES), F32),
            pltpu.VMEM((qs, tall, LANES), F32),
            pltpu.VMEM((tall, LANES), F32),
            pltpu.VMEM((qs, tall, LANES), F32),
            pltpu.VMEM((width, LANES), F32),
            pltpu.VMEM((zs, xys, per, LANES), F32),
            pltpu.VMEM((zs, xys, per, LANES), F32),
            pltpu.VMEM((xys, zs, per, LANES), F32),
            pltpu.VMEM((zs, per, LANES), F32),
            pltpu.VMEM((zs, per, LANES), F32),
            pltpu.VMEM((per, LANES), F32),
            pltpu.VMEM((2, xys, per, LANES), F32),
            pltpu.VMEM((qs, dates, sets), F32),
            dma((qs,)), dma((qs,)), dma((qs,)), dma((qs,)), dma, dma, dma((xys,)), dma((xys,)), dma((zs,)), dma((zs,)),
            dma((qs,)), dma((qs,)), dma((qs,)), dma((qs,)),
        ],
        compiler_params=pltpu.CompilerParams(
            collective_id=0, has_side_effects=True, vmem_limit_bytes=48 << 20
        ),
        name="exchange",
    )(netted.reshape(zs, 2, xys, per, LANES), gram, basis, weights.reshape(1, -1), thresholds.reshape(1, -1))


def body(
    start_state, shocks, loadings, strikes, notionals, trade_set, live_counts, weights, thresholds
):
    zs, qs = lax.axis_size("trade"), lax.axis_size("path")
    filled = live_counts[lax.axis_index("trade")]
    netted, gram, basis = local_moments(
        start_state, shocks, loadings, strikes, notionals, trade_set, filled, weights, thresholds.shape[0] * zs
    )
    return exchange(netted, gram, basis, weights, thresholds, zs, qs)


def solution(mesh):
    placed = (
        P("path", None),
        P(None, "path", None),
        P(None, "trade"),
        P("trade"),
        P("trade"),
        P("trade"),
        P(),
        P("path"),
        P("trade"),
    )
    return jax.shard_map(
        body,
        mesh=mesh,
        in_specs=placed,
        out_specs=(P(None, "trade", "path"), P(None, "trade")),
        check_vma=False,
    )
```

```python
import functools

import jax
import jax.numpy as jnp
from jax import lax
from jax.experimental import pallas as pl
from jax.experimental.pallas import tpu as pltpu
from jax.sharding import PartitionSpec as P

ROOT_HALF = 0.7071067811865476
F32, BF16 = jnp.float32, jnp.bfloat16
HIGHEST = lax.Precision.HIGHEST
MESH = pl.DeviceIdType.MESH
LANES = 128


def split(value):
    high = value.astype(BF16)
    return high, (value - high.astype(F32)).astype(BF16)


def dot(left, right, left_dim, right_dim, precision=None):
    return lax.dot_general(
        left, right, (((left_dim,), (right_dim,)), ((), ())), precision=precision, preferred_element_type=F32
    )


def make_basis(state):
    return jnp.concatenate([state, (state * state - 1.0) * ROOT_HALF], axis=0)


def scaled_trades(loadings_ref, strikes_ref, notionals_ref, block, size):
    cols = pl.ds(pl.multiple_of(block * size, size), size)
    scale = jnp.abs(notionals_ref[:, cols])
    high, low = split(loadings_ref[:, cols] * scale)
    strike = strikes_ref[:, cols] * (-scale)
    first = strike.astype(BF16).astype(F32)
    second = (strike - first).astype(BF16).astype(F32)
    third = (strike - first) - second
    row = lax.broadcasted_iota(jnp.int32, high.shape, 0)
    parts = jnp.where(row == 0, first, jnp.where(row == 1, second, jnp.where(row == 2, third, 0.0)))
    return jnp.concatenate([high, low, high, parts.astype(BF16)], axis=0)


def invert_steps(matrix_ref, begin, end):
    size = matrix_ref.shape[0]
    lane = lax.broadcasted_iota(jnp.int32, (size, LANES), 1)
    row_id = lax.broadcasted_iota(jnp.int32, (size, LANES), 0)
    lane_row = lax.broadcasted_iota(jnp.int32, (1, LANES), 1)

    def step(j, carry):
        matrix = matrix_ref[...]
        row = matrix_ref[pl.ds(j, 1), :]

        def pick(entries, ids):
            first = jnp.sum(jnp.where(ids == j, entries, 0.0), axis=1, keepdims=True)
            second = jnp.sum(jnp.where(ids == j + size, entries, 0.0), axis=1, keepdims=True)
            return jnp.where(ids < size, first, second)

        column = pick(matrix, lane)
        inverse = 1.0 / pick(row, lane_row)
        scaled = row * inverse
        here = jnp.logical_or(lane == j, lane == j + size)
        reduced = jnp.where(here, -column * inverse, matrix - column * scaled)
        pivot_row = jnp.where(jnp.logical_or(lane_row == j, lane_row == j + size), inverse, scaled)
        matrix_ref[...] = jnp.where(row_id == j, pivot_row, reduced)
        return carry

    lax.fori_loop(begin, end, step, 0)


def loop(begin, end, act):
    def step(i, carry):
        act(i)
        return carry

    lax.fori_loop(begin, end, step, 0)


def kernel(
    zs, xys, size,
    start_ref, shocks_ref, weights_ref, thresholds_ref, counts_ref, loadings_hbm, strikes_hbm, notionals_hbm, sets_hbm,
    exposure_ref, expected_ref,
    loadings_ref, strikes_ref, notionals_ref, sets_ref, local_sem,
    own_states, other_states, state_ref, wbasis_ref, basis_ref, moment_ref,
    gram_out, gram_in, gram_sum, gram_all, matrix_ref,
    net_ref, core_in, plane_out, plane_in, z_out, z_in, own_ref, coeffs_ref, part_ref,
    state_send, state_recv, gram_send, gram_recv, gall_send, gall_recv, core_send, core_recv, plane_send, plane_recv,
    z_send, z_recv, coeff_send, coeff_recv, part_send, part_recv,
):
    z = lax.axis_index("trade")
    q = lax.axis_index("path")
    xy, core = q // 2, lax.rem(q, 2)
    other = 1 - core
    qs = 2 * xys
    factors, paths = start_ref.shape
    dates = shocks_ref.shape[0]
    width = 2 * factors
    slots = loadings_ref.shape[1]
    chunks = core_send.shape[0]
    per_chunk = zs // chunks
    set_count = per_chunk * thresholds_ref.shape[1]

    def copy(src, dst, send, recv, device):
        return pltpu.make_async_remote_copy(
            src_ref=src, dst_ref=dst, send_sem=send, recv_sem=recv, device_id=device, device_id_type=MESH
        )

    half = pl.ds(pl.multiple_of(core * slots, slots), slots)
    fetches = [
        pltpu.make_async_copy(hbm.at[:, half], ref, local_sem.at[i])
        for i, (hbm, ref) in enumerate(
            [
                (loadings_hbm, loadings_ref),
                (strikes_hbm, strikes_ref),
                (notionals_hbm, notionals_ref),
                (sets_hbm, sets_ref),
            ]
        )
    ]
    for fetch in fetches:
        fetch.start()

    barrier = pltpu.get_barrier_semaphore()

    def greet(device):
        pl.semaphore_signal(barrier, inc=1, device_id=device, device_id_type=MESH)

    loop(1, qs, lambda o: greet((z, lax.rem(q + o, qs))))
    loop(1, zs, lambda o: greet((lax.rem(z + o, zs), q)))

    weight = jnp.broadcast_to(weights_ref[...].astype(F32), (8, paths))
    state = start_ref[...]
    own_states[0:factors, :] = state
    for date in range(dates):
        state = 0.8 * state + 0.6 * shocks_ref[date]
        own_states[(date + 1) * factors : (date + 2) * factors, :] = state
    bottom = (dates + 1) * factors
    own_states[bottom : bottom + 8, :] = weight

    pl.semaphore_wait(barrier, qs - 1 + zs - 1)
    states_copy = copy(own_states, other_states, state_send, state_recv, (z, xy * 2 + other))
    states_copy.start()

    def prepare(states, place):
        cols = pl.ds(place * paths, paths)
        scale = states[bottom : bottom + 1, :]
        grams = []
        for date in range(dates):
            basis = make_basis(states[date * factors : (date + 1) * factors, :])
            weighted = basis * scale
            high, low = split(weighted)
            wbasis_ref[date, 0:width, cols] = high
            wbasis_ref[date, width : 2 * width, cols] = low
            grams.append(dot(weighted, basis, 1, 1, HIGHEST))
            future = states[(date + 1) * factors : (date + 2) * factors, :]
            high = future.astype(BF16).astype(F32)
            ones = jnp.where(lax.broadcasted_iota(jnp.int32, future.shape, 0) < 3, 1.0, 0.0)
            rows = jnp.concatenate([high, high, future - high, ones], axis=0)
            state_ref[date, cols, :] = rows.T.astype(BF16)
            if place == 0:
                high, low = split(basis)
                zero = jnp.zeros_like(high)
                for part, entries in enumerate((high, high, low)):
                    for k in range(dates):
                        at = part * dates * width + k * width
                        basis_ref[date, at : at + width, :] = entries if k == date else zero
        return jnp.concatenate(grams, axis=1), jnp.sum(scale, axis=1, keepdims=True)

    gram, total = prepare(own_states, 0)
    states_copy.wait_recv()
    more, more_total = prepare(other_states, 1)
    gram = gram + more
    total = total + more_total

    rows = width // xys
    for piece in range(xys):
        gram_out[piece, 0:rows, :] = gram[piece * rows : (piece + 1) * rows, :]
        gram_out[piece, rows : rows + 1, :] = jnp.broadcast_to(total, (1, LANES))

    def plane_device(o):
        return (z, lax.rem(xy + o, xys) * 2 + core)

    def gram_copy(o):
        return copy(gram_out.at[lax.rem(xy + o, xys)], gram_in.at[o], gram_send.at[o], gram_recv.at[o], plane_device(o))

    loop(1, xys, lambda o: gram_copy(o).start())
    gram_in[0] = gram_out[xy]

    for fetch in fetches:
        fetch.wait()

    def moments(block):
        trades = scaled_trades(loadings_ref, strikes_ref, notionals_ref, block, size)
        cols = pl.ds(pl.multiple_of(block * size, size), size)
        for date in range(dates):
            flows = jnp.maximum(dot(state_ref[date], trades, 1, 0), 0.0)
            high, low = split(flows)
            both = dot(wbasis_ref[date], high, 1, 0)
            least = dot(wbasis_ref[date, 0:width, :], low, 1, 0)
            high, low = split(both[0:width] + both[width:] + least)
            moment_ref[date * width : (date + 1) * width, cols] = high
            moment_ref[LANES + date * width : LANES + (date + 1) * width, cols] = low

    loop(0, slots // size, moments)

    loop(1, xys, lambda o: gram_copy(o).wait_recv())
    gram_sum[...] = jnp.sum(gram_in[...], axis=0)

    def gall_copy(o):
        return copy(gram_sum, gram_all.at[xy], gall_send.at[o], gall_recv.at[o], plane_device(o))

    def gall_wait(o):
        return copy(gram_sum, gram_all.at[lax.rem(xy + xys - o, xys)], gall_send.at[o], gall_recv.at[o], plane_device(o))

    loop(1, xys, lambda o: gall_copy(o).start())
    gram_all[xy] = gram_sum[...]

    slot = core * slots + lax.broadcasted_iota(jnp.int32, (1, slots), 1)
    sets_ref[...] = jnp.where(slot < counts_ref[z], sets_ref[...], -1)
    notional = notionals_ref[...]
    notionals_ref[...] = jnp.where(notional > 0, 1.0, jnp.where(notional < 0, -1.0, 0.0))

    def owners(chunk):
        return pl.ds(chunk * per_chunk, per_chunk)

    def core_copy(chunk):
        return copy(
            net_ref.at[owners(chunk), other],
            core_in.at[owners(chunk)],
            core_send.at[chunk],
            core_recv.at[chunk],
            (z, xy * 2 + other),
        )

    def plane_copy(chunk, o):
        return copy(
            plane_out.at[owners(chunk), lax.rem(xy + o, xys)],
            plane_in.at[o, owners(chunk)],
            plane_send.at[chunk, o],
            plane_recv.at[chunk, o],
            plane_device(o),
        )

    def to_plane(chunk):
        core_copy(chunk).wait_recv()
        plane_out[owners(chunk)] = net_ref[owners(chunk), core] + core_in[owners(chunk)]
        loop(1, xys, lambda o: plane_copy(chunk, o).start())
        plane_in[0, owners(chunk)] = plane_out[owners(chunk), xy]

    def net(chunk):
        row = lax.broadcasted_iota(jnp.int32, (set_count, slots), 0) + chunk * set_count
        member = jnp.where(row == sets_ref[...], notionals_ref[...], 0.0).astype(BF16)
        both = dot(member, moment_ref[...], 1, 1)
        net_ref[owners(chunk)] = (both[:, :LANES] + both[:, LANES:]).reshape(per_chunk, *net_ref.shape[1:])
        core_copy(chunk).start()

        @pl.when(chunk > 0)
        def _():
            to_plane(chunk - 1)

    loop(0, chunks, net)
    to_plane(chunks - 1)

    def z_copy(to):
        return copy(z_out.at[to], z_in.at[z], z_send.at[to], z_recv.at[z], (to, q))

    def z_wait(src):
        return copy(z_out.at[src], z_in.at[src], z_send.at[src], z_recv.at[src], (src, q))

    def others(act):
        def one(to):
            @pl.when(to != z)
            def _():
                act(to)

        return one

    def to_z(chunk):
        loop(1, xys, lambda o: plane_copy(chunk, o).wait_recv())
        z_out[owners(chunk)] = jnp.sum(plane_in[:, owners(chunk)], axis=0)
        loop(chunk * per_chunk, (chunk + 1) * per_chunk, others(lambda to: z_copy(to).start()))

    loop(0, chunks - 1, to_z)
    loop(1, xys, lambda o: gall_wait(o).wait_recv())
    for piece in range(xys):
        matrix_ref[piece * rows : (piece + 1) * rows, :] = gram_all[piece, 0:rows, :]
    invert_steps(matrix_ref, 0, width // 2)
    to_z(chunks - 1)
    z_in[z] = z_out[z]
    invert_steps(matrix_ref, width // 2, width)
    inverse = matrix_ref[...]
    left = lax.broadcasted_iota(jnp.int32, inverse.shape, 1) < width
    block = jnp.concatenate([jnp.where(left, inverse, 0.0), jnp.where(left, 0.0, inverse)], axis=0)
    loop(0, zs, others(lambda src: z_wait(src).wait_recv()))
    own_ref[...] = dot(jnp.sum(z_in[...], axis=0), block, 1, 0, HIGHEST)

    def any_device(o):
        return (z, lax.rem(q + o, qs))

    def coeff_copy(o):
        return copy(own_ref, coeffs_ref.at[core, xy], coeff_send.at[o], coeff_recv.at[o], any_device(o))

    def coeff_wait(o):
        src = lax.rem(q + qs - o, qs)
        return copy(
            own_ref, coeffs_ref.at[lax.rem(src, 2), src // 2], coeff_send.at[o], coeff_recv.at[o], any_device(o)
        )

    loop(1, qs, lambda o: coeff_copy(o).start())
    coeffs_ref[core, xy] = own_ref[...]
    sets = thresholds_ref.shape[1]
    limits = jnp.broadcast_to(0.25 * thresholds_ref[...].astype(F32), (LANES, sets)).T
    loop(1, qs, lambda o: coeff_wait(o).wait_recv())

    high, low = split(coeffs_ref[...].reshape(sets, LANES))
    coeffs = jnp.concatenate([high, low, high], axis=1)
    weight = weight.astype(BF16)
    for date in range(dates):
        exposure = jnp.maximum(dot(coeffs, basis_ref[date], 1, 0) - limits[:, 0:1], 0.0)
        exposure_ref[date] = exposure
        high, low = split(exposure)
        part = dot(weight, high, 1, 1) + dot(weight, low, 1, 1)
        part_ref[q, date : date + 1, :] = part[0:1, :]

    def part_copy(o):
        return copy(part_ref.at[q], part_ref.at[q], part_send.at[o], part_recv.at[o], any_device(o))

    def part_wait(o):
        src = lax.rem(q + qs - o, qs)
        return copy(part_ref.at[q], part_ref.at[src], part_send.at[o], part_recv.at[o], any_device(o))

    loop(1, qs, lambda o: part_copy(o).start())
    states_copy.wait_send()
    loop(1, xys, lambda o: gram_copy(o).wait_send())
    loop(1, xys, lambda o: gall_copy(o).wait_send())
    loop(0, chunks, lambda chunk: core_copy(chunk).wait_send())
    loop(0, chunks, lambda chunk: loop(1, xys, lambda o: plane_copy(chunk, o).wait_send()))
    loop(0, zs, others(lambda to: z_copy(to).wait_send()))
    loop(1, qs, lambda o: coeff_copy(o).wait_send())
    loop(1, qs, lambda o: part_wait(o).wait_recv())
    expected_ref[...] = jnp.sum(part_ref[...], axis=0) / gram_all[0, rows : rows + 1, 0:1]
    loop(1, qs, lambda o: part_copy(o).wait_send())


def body(
    start_state, shocks, loadings, strikes, notionals, trade_set, live_counts, weights, thresholds
):
    zs, qs = lax.axis_size("trade"), lax.axis_size("path")
    xys = qs // 2
    paths, factors = start_state.shape
    dates = shocks.shape[0]
    width = 2 * factors
    slots = loadings.shape[1] // 2
    size = min(1024, slots)
    sets = thresholds.shape[0]
    per = sets // qs
    chunks = 4 if zs % 4 == 0 else zs
    tall = (width // xys + 8) // 8 * 8
    vmem = pl.BlockSpec(memory_space=pltpu.VMEM)
    hbm = pl.BlockSpec(memory_space=pl.ANY)
    dma = pltpu.SemaphoreType.DMA
    return pl.pallas_call(
        functools.partial(kernel, zs, xys, size),
        out_shape=(
            jax.ShapeDtypeStruct((dates, sets, paths), F32),
            jax.ShapeDtypeStruct((dates, sets), F32),
        ),
        in_specs=[vmem] * 4 + [pl.BlockSpec(memory_space=pltpu.SMEM)] + [hbm] * 4,
        out_specs=(vmem, vmem),
        scratch_shapes=[
            pltpu.VMEM((factors, slots), F32),
            pltpu.VMEM((1, slots), F32),
            pltpu.VMEM((1, slots), F32),
            pltpu.VMEM((1, slots), jnp.int32),
            dma((4,)),
            pltpu.VMEM(((dates + 1) * factors + 8, paths), F32),
            pltpu.VMEM(((dates + 1) * factors + 8, paths), F32),
            pltpu.VMEM((dates, 2 * paths, 4 * factors), BF16),
            pltpu.VMEM((dates, 2 * width, 2 * paths), BF16),
            pltpu.VMEM((dates, 3 * dates * width, paths), BF16),
            pltpu.VMEM((2 * LANES, slots), BF16),
            pltpu.VMEM((xys, tall, LANES), F32),
            pltpu.VMEM((xys, tall, LANES), F32),
            pltpu.VMEM((tall, LANES), F32),
            pltpu.VMEM((xys, tall, LANES), F32),
            pltpu.VMEM((width, LANES), F32),
            pltpu.VMEM((zs, 2, xys, per, LANES), F32),
            pltpu.VMEM((zs, xys, per, LANES), F32),
            pltpu.VMEM((zs, xys, per, LANES), F32),
            pltpu.VMEM((xys, zs, per, LANES), F32),
            pltpu.VMEM((zs, per, LANES), F32),
            pltpu.VMEM((zs, per, LANES), F32),
            pltpu.VMEM((per, LANES), F32),
            pltpu.VMEM((2, xys, per, LANES), F32),
            pltpu.VMEM((qs, dates, sets), F32),
            dma, dma, dma((xys,)), dma((xys,)), dma((xys,)), dma((xys,)), dma((chunks,)), dma((chunks,)),
            dma((chunks, xys)), dma((chunks, xys)), dma((zs,)), dma((zs,)), dma((qs,)), dma((qs,)), dma((qs,)), dma((qs,)),
        ],
        compiler_params=pltpu.CompilerParams(
            collective_id=0, has_side_effects=True, vmem_limit_bytes=56 << 20
        ),
        name="exposures",
    )(
        start_state.T, shocks.transpose(0, 2, 1), weights.reshape(1, -1), thresholds.reshape(1, -1), live_counts,
        loadings, strikes.reshape(1, -1), notionals.reshape(1, -1), trade_set.reshape(1, -1),
    )


def solution(mesh):
    placed = (
        P("path", None),
        P(None, "path", None),
        P(None, "trade"),
        P("trade"),
        P("trade"),
        P("trade"),
        P(),
        P("path"),
        P("trade"),
    )
    return jax.shard_map(
        body,
        mesh=mesh,
        in_specs=placed,
        out_specs=(P(None, "trade", "path"), P(None, "trade")),
        check_vma=False,
    )
```

```python
import functools

import jax
import jax.numpy as jnp
from jax import lax
from jax.experimental import pallas as pl
from jax.experimental.pallas import tpu as pltpu
from jax.sharding import PartitionSpec as P

ROOT_HALF = 0.7071067811865476
F32, BF16 = jnp.float32, jnp.bfloat16
HIGHEST = lax.Precision.HIGHEST
MESH = pl.DeviceIdType.MESH
LANES = 128


def split(value):
    high = value.astype(BF16)
    return high, (value - high.astype(F32)).astype(BF16)


def dot(left, right, left_dim, right_dim, precision=None):
    return lax.dot_general(
        left, right, (((left_dim,), (right_dim,)), ((), ())), precision=precision, preferred_element_type=F32
    )


def make_basis(state):
    return jnp.concatenate([state, (state * state - 1.0) * ROOT_HALF], axis=0)


def scaled_trades(loadings_ref, strikes_ref, notionals_ref, block, size):
    cols = pl.ds(pl.multiple_of(block * size, size), size)
    scale = jnp.abs(notionals_ref[:, cols])
    high, low = split(loadings_ref[:, cols] * scale)
    strike = strikes_ref[:, cols] * (-scale)
    first = strike.astype(BF16).astype(F32)
    second = (strike - first).astype(BF16).astype(F32)
    third = (strike - first) - second
    row = lax.broadcasted_iota(jnp.int32, high.shape, 0)
    parts = jnp.where(row == 0, first, jnp.where(row == 1, second, jnp.where(row == 2, third, 0.0)))
    return jnp.concatenate([high, low, high, parts.astype(BF16)], axis=0)


def invert_steps(matrix_ref, begin, count):
    size = matrix_ref.shape[0]
    lane = lax.broadcasted_iota(jnp.int32, (size, LANES), 1)
    row_id = lax.broadcasted_iota(jnp.int32, (size, LANES), 0)
    lane_row = lax.broadcasted_iota(jnp.int32, (1, LANES), 1)

    for j in [begin + i for i in range(count)]:
        matrix = matrix_ref[...]
        row = matrix_ref[pl.ds(j, 1), :]

        def pick(entries, ids, j=j):
            first = jnp.sum(jnp.where(ids == j, entries, 0.0), axis=1, keepdims=True)
            second = jnp.sum(jnp.where(ids == j + size, entries, 0.0), axis=1, keepdims=True)
            return jnp.where(ids < size, first, second)

        column = pick(matrix, lane)
        inverse = 1.0 / pick(row, lane_row)
        scaled = row * inverse
        here = jnp.logical_or(lane == j, lane == j + size)
        reduced = jnp.where(here, -column * inverse, matrix - column * scaled)
        pivot_row = jnp.where(jnp.logical_or(lane_row == j, lane_row == j + size), inverse, scaled)
        matrix_ref[...] = jnp.where(row_id == j, pivot_row, reduced)


def loop(begin, end, act):
    def step(i, carry):
        act(i)
        return carry

    lax.fori_loop(begin, end, step, 0)


def kernel(
    zs, xys, size,
    start_ref, shocks_ref, weights_ref, thresholds_ref, counts_ref, loadings_hbm, strikes_hbm, notionals_hbm, sets_hbm,
    exposure_ref, expected_ref,
    loadings_ref, strikes_ref, notionals_ref, sets_ref, local_sem,
    own_states, other_states, state_ref, wbasis_ref, basis_ref, moment_ref,
    gram_out, gram_in, gram_sum, gram_all, matrix_ref,
    net_ref, core_in, plane_out, plane_in, z_out, z_in, own_ref, coeffs_ref, part_ref,
    state_send, state_recv, gram_send, gram_recv, gall_send, gall_recv, core_send, core_recv, plane_send, plane_recv,
    z_send, z_recv, coeff_send, coeff_recv, part_send, part_recv,
):
    z = lax.axis_index("trade")
    q = lax.axis_index("path")
    xy, core = q // 2, lax.rem(q, 2)
    other = 1 - core
    qs = 2 * xys
    factors, paths = start_ref.shape
    dates = shocks_ref.shape[0]
    width = 2 * factors
    slots = loadings_ref.shape[1]
    chunks = core_send.shape[0]
    per_chunk = zs // chunks
    set_count = per_chunk * thresholds_ref.shape[1]

    def copy(src, dst, send, recv, device):
        return pltpu.make_async_remote_copy(
            src_ref=src, dst_ref=dst, send_sem=send, recv_sem=recv, device_id=device, device_id_type=MESH
        )

    half = pl.ds(pl.multiple_of(core * slots, slots), slots)
    fetches = [
        pltpu.make_async_copy(hbm.at[:, half], ref, local_sem.at[i])
        for i, (hbm, ref) in enumerate(
            [
                (loadings_hbm, loadings_ref),
                (strikes_hbm, strikes_ref),
                (notionals_hbm, notionals_ref),
                (sets_hbm, sets_ref),
            ]
        )
    ]
    for fetch in fetches:
        fetch.start()

    barrier = pltpu.get_barrier_semaphore()

    def greet(device):
        pl.semaphore_signal(barrier, inc=1, device_id=device, device_id_type=MESH)

    loop(1, qs, lambda o: greet((z, lax.rem(q + o, qs))))
    loop(1, zs, lambda o: greet((lax.rem(z + o, zs), q)))

    weight = jnp.broadcast_to(weights_ref[...].astype(F32), (8, paths))
    state = start_ref[...]
    own_states[0:factors, :] = state
    for date in range(dates):
        state = 0.8 * state + 0.6 * shocks_ref[date]
        own_states[(date + 1) * factors : (date + 2) * factors, :] = state
    bottom = (dates + 1) * factors
    own_states[bottom : bottom + 8, :] = weight

    pl.semaphore_wait(barrier, qs - 1 + zs - 1)
    states_copy = copy(own_states, other_states, state_send, state_recv, (z, xy * 2 + other))
    states_copy.start()

    def prepare(states, place):
        cols = pl.ds(place * paths, paths)
        scale = states[bottom : bottom + 1, :]
        grams = []
        for date in range(dates):
            basis = make_basis(states[date * factors : (date + 1) * factors, :])
            weighted = basis * scale
            high, low = split(weighted)
            wbasis_ref[date, 0:width, cols] = high
            wbasis_ref[date, width : 2 * width, cols] = low
            grams.append(dot(weighted, basis, 1, 1, HIGHEST))
            future = states[(date + 1) * factors : (date + 2) * factors, :]
            high = future.astype(BF16).astype(F32)
            ones = jnp.where(lax.broadcasted_iota(jnp.int32, future.shape, 0) < 3, 1.0, 0.0)
            rows = jnp.concatenate([high, high, future - high, ones], axis=0)
            state_ref[date, cols, :] = rows.T.astype(BF16)
            if place == 0:
                high, low = split(basis)
                zero = jnp.zeros_like(high)
                for part, entries in enumerate((high, high, low)):
                    for k in range(dates):
                        at = part * dates * width + k * width
                        basis_ref[date, at : at + width, :] = entries if k == date else zero
        return jnp.concatenate(grams, axis=1), jnp.sum(scale, axis=1, keepdims=True)

    gram, total = prepare(own_states, 0)
    states_copy.wait_recv()
    more, more_total = prepare(other_states, 1)
    gram = gram + more
    total = total + more_total

    rows = width // xys
    for piece in range(xys):
        gram_out[piece, 0:rows, :] = gram[piece * rows : (piece + 1) * rows, :]
        gram_out[piece, rows : rows + 1, :] = jnp.broadcast_to(total, (1, LANES))

    def plane_device(o):
        return (z, lax.rem(xy + o, xys) * 2 + core)

    def gram_copy(o):
        return copy(gram_out.at[lax.rem(xy + o, xys)], gram_in.at[o], gram_send.at[o], gram_recv.at[o], plane_device(o))

    loop(1, xys, lambda o: gram_copy(o).start())
    gram_in[0] = gram_out[xy]

    for fetch in fetches:
        fetch.wait()

    def moments(block):
        trades = scaled_trades(loadings_ref, strikes_ref, notionals_ref, block, size)
        cols = pl.ds(pl.multiple_of(block * size, size), size)
        for date in range(dates):
            flows = jnp.maximum(dot(state_ref[date], trades, 1, 0), 0.0)
            high, low = split(flows)
            both = dot(wbasis_ref[date], high, 1, 0)
            least = dot(wbasis_ref[date, 0:width, :], low, 1, 0)
            high, low = split(both[0:width] + both[width:] + least)
            moment_ref[date * width : (date + 1) * width, cols] = high
            moment_ref[LANES + date * width : LANES + (date + 1) * width, cols] = low

    blocks = slots // size
    loop(0, blocks // 2, moments)

    loop(1, xys, lambda o: gram_copy(o).wait_recv())
    gram_sum[...] = jnp.sum(gram_in[...], axis=0)

    def gall_copy(o):
        return copy(gram_sum, gram_all.at[xy], gall_send.at[o], gall_recv.at[o], plane_device(o))

    def gall_wait(o):
        return copy(gram_sum, gram_all.at[lax.rem(xy + xys - o, xys)], gall_send.at[o], gall_recv.at[o], plane_device(o))

    loop(1, xys, lambda o: gall_copy(o).start())
    gram_all[xy] = gram_sum[...]

    loop(blocks // 2, blocks, moments)

    loop(1, xys, lambda o: gall_wait(o).wait_recv())
    for piece in range(xys):
        matrix_ref[piece * rows : (piece + 1) * rows, :] = gram_all[piece, 0:rows, :]

    slot = core * slots + lax.broadcasted_iota(jnp.int32, (1, slots), 1)
    sets_ref[...] = jnp.where(slot < counts_ref[z], sets_ref[...], -1)
    notional = notionals_ref[...]
    notionals_ref[...] = jnp.where(notional > 0, 1.0, jnp.where(notional < 0, -1.0, 0.0))

    def owners(chunk):
        return pl.ds(chunk * per_chunk, per_chunk)

    def core_copy(chunk):
        return copy(
            net_ref.at[owners(chunk), other],
            core_in.at[owners(chunk)],
            core_send.at[chunk],
            core_recv.at[chunk],
            (z, xy * 2 + other),
        )

    def plane_copy(chunk, o):
        return copy(
            plane_out.at[owners(chunk), lax.rem(xy + o, xys)],
            plane_in.at[o, owners(chunk)],
            plane_send.at[chunk, o],
            plane_recv.at[chunk, o],
            plane_device(o),
        )

    def to_plane(chunk):
        core_copy(chunk).wait_recv()
        plane_out[owners(chunk)] = net_ref[owners(chunk), core] + core_in[owners(chunk)]
        loop(1, xys, lambda o: plane_copy(chunk, o).start())
        plane_in[0, owners(chunk)] = plane_out[owners(chunk), xy]

    def net(chunk):
        row = lax.broadcasted_iota(jnp.int32, (set_count, slots), 0) + chunk * set_count
        member = jnp.where(row == sets_ref[...], notionals_ref[...], 0.0).astype(BF16)
        both = dot(member, moment_ref[...], 1, 1)
        invert_steps(matrix_ref, chunk * (width // chunks), width // chunks)
        net_ref[owners(chunk)] = (both[:, :LANES] + both[:, LANES:]).reshape(per_chunk, *net_ref.shape[1:])
        core_copy(chunk).start()

        @pl.when(chunk > 0)
        def _():
            to_plane(chunk - 1)

    loop(0, chunks, net)
    to_plane(chunks - 1)

    def z_copy(to):
        return copy(z_out.at[to], z_in.at[z], z_send.at[to], z_recv.at[z], (to, q))

    def z_wait(src):
        return copy(z_out.at[src], z_in.at[src], z_send.at[src], z_recv.at[src], (src, q))

    def others(act):
        def one(to):
            @pl.when(to != z)
            def _():
                act(to)

        return one

    def to_z(chunk):
        loop(1, xys, lambda o: plane_copy(chunk, o).wait_recv())
        z_out[owners(chunk)] = jnp.sum(plane_in[:, owners(chunk)], axis=0)
        loop(chunk * per_chunk, (chunk + 1) * per_chunk, others(lambda to: z_copy(to).start()))

    loop(0, chunks, to_z)
    z_in[z] = z_out[z]
    inverse = matrix_ref[...]
    left = lax.broadcasted_iota(jnp.int32, inverse.shape, 1) < width
    block = jnp.concatenate([jnp.where(left, inverse, 0.0), jnp.where(left, 0.0, inverse)], axis=0)
    loop(0, zs, others(lambda src: z_wait(src).wait_recv()))
    own_ref[...] = dot(jnp.sum(z_in[...], axis=0), block, 1, 0, HIGHEST)

    def any_device(o):
        return (z, lax.rem(q + o, qs))

    def coeff_copy(o):
        return copy(own_ref, coeffs_ref.at[core, xy], coeff_send.at[o], coeff_recv.at[o], any_device(o))

    def coeff_wait(o):
        src = lax.rem(q + qs - o, qs)
        return copy(
            own_ref, coeffs_ref.at[lax.rem(src, 2), src // 2], coeff_send.at[o], coeff_recv.at[o], any_device(o)
        )

    loop(1, qs, lambda o: coeff_copy(o).start())
    coeffs_ref[core, xy] = own_ref[...]
    sets = thresholds_ref.shape[1]
    limits = jnp.broadcast_to(0.25 * thresholds_ref[...].astype(F32), (LANES, sets)).T
    loop(1, qs, lambda o: coeff_wait(o).wait_recv())

    high, low = split(coeffs_ref[...].reshape(sets, LANES))
    coeffs = jnp.concatenate([high, low, high], axis=1)
    weight = weight.astype(BF16)
    for date in range(dates):
        exposure = jnp.maximum(dot(coeffs, basis_ref[date], 1, 0) - limits[:, 0:1], 0.0)
        exposure_ref[date] = exposure
        high, low = split(exposure)
        part = dot(weight, high, 1, 1) + dot(weight, low, 1, 1)
        part_ref[q, date : date + 1, :] = part[0:1, :]

    def part_copy(o):
        return copy(part_ref.at[q], part_ref.at[q], part_send.at[o], part_recv.at[o], any_device(o))

    def part_wait(o):
        src = lax.rem(q + qs - o, qs)
        return copy(part_ref.at[q], part_ref.at[src], part_send.at[o], part_recv.at[o], any_device(o))

    loop(1, qs, lambda o: part_copy(o).start())
    states_copy.wait_send()
    loop(1, xys, lambda o: gram_copy(o).wait_send())
    loop(1, xys, lambda o: gall_copy(o).wait_send())
    loop(0, chunks, lambda chunk: core_copy(chunk).wait_send())
    loop(0, chunks, lambda chunk: loop(1, xys, lambda o: plane_copy(chunk, o).wait_send()))
    loop(0, zs, others(lambda to: z_copy(to).wait_send()))
    loop(1, qs, lambda o: coeff_copy(o).wait_send())
    loop(1, qs, lambda o: part_wait(o).wait_recv())
    expected_ref[...] = jnp.sum(part_ref[...], axis=0) / gram_all[0, rows : rows + 1, 0:1]
    loop(1, qs, lambda o: part_copy(o).wait_send())


def body(
    start_state, shocks, loadings, strikes, notionals, trade_set, live_counts, weights, thresholds
):
    zs, qs = lax.axis_size("trade"), lax.axis_size("path")
    xys = qs // 2
    paths, factors = start_state.shape
    dates = shocks.shape[0]
    width = 2 * factors
    slots = loadings.shape[1] // 2
    size = min(1024, slots)
    sets = thresholds.shape[0]
    per = sets // qs
    chunks = 4 if zs % 4 == 0 else zs
    tall = (width // xys + 8) // 8 * 8
    vmem = pl.BlockSpec(memory_space=pltpu.VMEM)
    hbm = pl.BlockSpec(memory_space=pl.ANY)
    dma = pltpu.SemaphoreType.DMA
    return pl.pallas_call(
        functools.partial(kernel, zs, xys, size),
        out_shape=(
            jax.ShapeDtypeStruct((dates, sets, paths), F32),
            jax.ShapeDtypeStruct((dates, sets), F32),
        ),
        in_specs=[vmem] * 4 + [pl.BlockSpec(memory_space=pltpu.SMEM)] + [hbm] * 4,
        out_specs=(vmem, vmem),
        scratch_shapes=[
            pltpu.VMEM((factors, slots), F32),
            pltpu.VMEM((1, slots), F32),
            pltpu.VMEM((1, slots), F32),
            pltpu.VMEM((1, slots), jnp.int32),
            dma((4,)),
            pltpu.VMEM(((dates + 1) * factors + 8, paths), F32),
            pltpu.VMEM(((dates + 1) * factors + 8, paths), F32),
            pltpu.VMEM((dates, 2 * paths, 4 * factors), BF16),
            pltpu.VMEM((dates, 2 * width, 2 * paths), BF16),
            pltpu.VMEM((dates, 3 * dates * width, paths), BF16),
            pltpu.VMEM((2 * LANES, slots), BF16),
            pltpu.VMEM((xys, tall, LANES), F32),
            pltpu.VMEM((xys, tall, LANES), F32),
            pltpu.VMEM((tall, LANES), F32),
            pltpu.VMEM((xys, tall, LANES), F32),
            pltpu.VMEM((width, LANES), F32),
            pltpu.VMEM((zs, 2, xys, per, LANES), F32),
            pltpu.VMEM((zs, xys, per, LANES), F32),
            pltpu.VMEM((zs, xys, per, LANES), F32),
            pltpu.VMEM((xys, zs, per, LANES), F32),
            pltpu.VMEM((zs, per, LANES), F32),
            pltpu.VMEM((zs, per, LANES), F32),
            pltpu.VMEM((per, LANES), F32),
            pltpu.VMEM((2, xys, per, LANES), F32),
            pltpu.VMEM((qs, dates, sets), F32),
            dma, dma, dma((xys,)), dma((xys,)), dma((xys,)), dma((xys,)), dma((chunks,)), dma((chunks,)),
            dma((chunks, xys)), dma((chunks, xys)), dma((zs,)), dma((zs,)), dma((qs,)), dma((qs,)), dma((qs,)), dma((qs,)),
        ],
        compiler_params=pltpu.CompilerParams(
            collective_id=0, has_side_effects=True, vmem_limit_bytes=56 << 20
        ),
        name="exposures",
    )(
        start_state.T, shocks.transpose(0, 2, 1), weights.reshape(1, -1), thresholds.reshape(1, -1), live_counts,
        loadings, strikes.reshape(1, -1), notionals.reshape(1, -1), trade_set.reshape(1, -1),
    )


def solution(mesh):
    placed = (
        P("path", None),
        P(None, "path", None),
        P(None, "trade"),
        P("trade"),
        P("trade"),
        P("trade"),
        P(),
        P("path"),
        P("trade"),
    )
    return jax.shard_map(
        body,
        mesh=mesh,
        in_specs=placed,
        out_specs=(P(None, "trade", "path"), P(None, "trade")),
        check_vma=False,
    )
```

```python
import functools

import jax
import jax.numpy as jnp
from jax import lax
from jax.experimental import pallas as pl
from jax.experimental.pallas import tpu as pltpu
from jax.sharding import PartitionSpec as P

ROOT_HALF = 0.7071067811865476
F32, BF16 = jnp.float32, jnp.bfloat16
HIGHEST = lax.Precision.HIGHEST
MESH = pl.DeviceIdType.MESH
LANES = 128


def split(value):
    high = value.astype(BF16)
    return high, (value - high.astype(F32)).astype(BF16)


def dot(left, right, left_dim, right_dim, precision=None):
    return lax.dot_general(
        left, right, (((left_dim,), (right_dim,)), ((), ())), precision=precision, preferred_element_type=F32
    )


def make_basis(state):
    return jnp.concatenate([state, (state * state - 1.0) * ROOT_HALF], axis=0)


def scaled_trades(loadings_ref, strikes_ref, notionals_ref, block, size):
    cols = pl.ds(pl.multiple_of(block * size, size), size)
    scale = jnp.abs(notionals_ref[:, cols])
    high, low = split(loadings_ref[:, cols] * scale)
    strike = strikes_ref[:, cols] * (-scale)
    first = strike.astype(BF16).astype(F32)
    second = (strike - first).astype(BF16).astype(F32)
    third = (strike - first) - second
    row = lax.broadcasted_iota(jnp.int32, high.shape, 0)
    parts = jnp.where(row == 0, first, jnp.where(row == 1, second, jnp.where(row == 2, third, 0.0)))
    return jnp.concatenate([high, low, high, parts.astype(BF16)], axis=0)


def invert_steps(matrix_ref, begin, count):
    size = matrix_ref.shape[0]
    lane = lax.broadcasted_iota(jnp.int32, (size, LANES), 1)
    row_id = lax.broadcasted_iota(jnp.int32, (size, LANES), 0)
    lane_row = lax.broadcasted_iota(jnp.int32, (1, LANES), 1)

    for j in [begin + i for i in range(count)]:
        matrix = matrix_ref[...]
        row = matrix_ref[pl.ds(j, 1), :]

        def pick(entries, ids, j=j):
            first = jnp.sum(jnp.where(ids == j, entries, 0.0), axis=1, keepdims=True)
            second = jnp.sum(jnp.where(ids == j + size, entries, 0.0), axis=1, keepdims=True)
            return jnp.where(ids < size, first, second)

        column = pick(matrix, lane)
        inverse = 1.0 / pick(row, lane_row)
        scaled = row * inverse
        here = jnp.logical_or(lane == j, lane == j + size)
        reduced = jnp.where(here, -column * inverse, matrix - column * scaled)
        pivot_row = jnp.where(jnp.logical_or(lane_row == j, lane_row == j + size), inverse, scaled)
        matrix_ref[...] = jnp.where(row_id == j, pivot_row, reduced)


def loop(begin, end, act):
    def step(i, carry):
        act(i)
        return carry

    lax.fori_loop(begin, end, step, 0)


def kernel(
    zs, xys, size,
    start_hbm, shocks_hbm, weights_hbm, thresholds_hbm, counts_ref, loadings_hbm, strikes_hbm, notionals_hbm, sets_hbm,
    exposure_ref, expected_ref,
    start_ref, shocks_ref, weights_ref, thresholds_ref,
    loadings_ref, strikes_ref, notionals_ref, sets_ref, local_sem, out_ref, out_sem,
    own_states, other_states, state_ref, wbasis_ref, basis_ref, total_ref, moment_ref,
    gram_out, gram_in, gram_sum, gram_all, matrix_ref,
    net_ref, core_in, plane_out, plane_in, z_out, z_in, own_ref, coeffs_ref, part_ref,
    state_send, state_recv, gram_send, gram_recv, gall_send, gall_recv, core_send, core_recv, plane_send, plane_recv,
    z_send, z_recv, coeff_send, coeff_recv, part_send, part_recv,
):
    z = lax.axis_index("trade")
    q = lax.axis_index("path")
    xy, core = q // 2, lax.rem(q, 2)
    other = 1 - core
    qs = 2 * xys
    factors, paths = start_ref.shape
    dates = shocks_ref.shape[0]
    width = 2 * factors
    slots = loadings_ref.shape[1]
    chunks = core_send.shape[0]
    per_chunk = zs // chunks
    set_count = per_chunk * thresholds_ref.shape[1]

    def copy(src, dst, send, recv, device):
        return pltpu.make_async_remote_copy(
            src_ref=src, dst_ref=dst, send_sem=send, recv_sem=recv, device_id=device, device_id_type=MESH
        )

    def target(cores, o):
        return (z, lax.rem(q + o, qs) if cores == 2 else lax.rem(xy + o, xys) * 2 + core)

    def wait_all(ref, send, recv):
        copy(ref, ref, send, recv, target(2, 1)).wait_recv()

    def sent_all(ref, send, recv):
        copy(ref, ref, send, recv, target(2, 1)).wait_send()

    def around(cores, act):
        loop(1, cores * xys, lambda o: act(o, cores, o))

    half = pl.ds(pl.multiple_of(core * slots, slots), slots)
    fetches = [
        pltpu.make_async_copy(hbm.at[:, half], ref, local_sem.at[i])
        for i, (hbm, ref) in enumerate(
            [
                (loadings_hbm, loadings_ref),
                (strikes_hbm, strikes_ref),
                (notionals_hbm, notionals_ref),
                (sets_hbm, sets_ref),
            ]
        )
    ]
    firsts = [
        pltpu.make_async_copy(hbm, ref, local_sem.at[len(fetches) + i])
        for i, (hbm, ref) in enumerate(
            [
                (start_hbm, start_ref),
                (shocks_hbm, shocks_ref),
                (weights_hbm, weights_ref),
                (thresholds_hbm, thresholds_ref),
            ]
        )
    ]
    for fetch in firsts + fetches:
        fetch.start()

    barrier = pltpu.get_barrier_semaphore()

    def greet(device):
        pl.semaphore_signal(barrier, inc=1, device_id=device, device_id_type=MESH)

    loop(1, qs, lambda o: greet((z, lax.rem(q + o, qs))))
    loop(1, zs, lambda o: greet((lax.rem(z + o, zs), q)))

    for fetch in firsts:
        fetch.wait()
    weight = jnp.broadcast_to(weights_ref[...].astype(F32), (8, paths))
    state = start_ref[...]
    own_states[0:factors, :] = state
    for date in range(dates):
        state = 0.8 * state + 0.6 * shocks_ref[date]
        own_states[(date + 1) * factors : (date + 2) * factors, :] = state
    bottom = (dates + 1) * factors
    own_states[bottom : bottom + 8, :] = weight

    def prepare(states, place):
        scale = states[bottom : bottom + 1, :]
        grams = []
        for date in range(dates):
            basis = make_basis(states[date * factors : (date + 1) * factors, :])
            weighted = basis * scale
            high, low = split(weighted)
            wbasis_ref[place, date, 0:width, :] = high
            wbasis_ref[place, date, width : 2 * width, :] = low
            future = states[(date + 1) * factors : (date + 2) * factors, :]
            high = future.astype(BF16).astype(F32)
            ones = jnp.where(lax.broadcasted_iota(jnp.int32, future.shape, 0) < 3, 1.0, 0.0)
            rows = jnp.concatenate([high, high, future - high, ones], axis=0)
            state_ref[place, date] = rows.T.astype(BF16)
            if place == 0:
                grams.append(dot(weighted, basis, 1, 1, HIGHEST))
                high, low = split(basis)
                zero = jnp.zeros_like(high)
                for part, entries in enumerate((high, high, low)):
                    for k in range(dates):
                        at = part * dates * width + k * width
                        basis_ref[date, at : at + width, :] = entries if k == date else zero
        return grams

    def moments(block, place):
        trades = scaled_trades(loadings_ref, strikes_ref, notionals_ref, block, size)
        cols = pl.ds(pl.multiple_of(block * size, size), size)
        for date in range(dates):
            flows = jnp.maximum(dot(state_ref[place, date], trades, 1, 0), 0.0)
            high, low = split(flows)
            both = dot(wbasis_ref[place, date], high, 1, 0)
            least = dot(wbasis_ref[place, date, 0:width, :], low, 1, 0)
            moment = both[0:width] + both[width:] + least
            at = date * width
            if place == 0:
                total_ref[at : at + width, cols] = moment
            else:
                high, low = split(moment + total_ref[at : at + width, cols])
                moment_ref[at : at + width, cols] = high
                moment_ref[LANES + at : LANES + at + width, cols] = low

    gram = jnp.concatenate(prepare(own_states, 0), axis=1)
    rows = width // qs
    for piece in range(qs):
        gram_out[piece, 0:rows, :] = gram[piece * rows : (piece + 1) * rows, :]
        gram_out[piece, rows : rows + 1, :] = jnp.broadcast_to(jnp.sum(weight[0:1, :], axis=1, keepdims=True), (1, LANES))
    for fetch in fetches:
        fetch.wait()
    blocks = slots // size
    loop(0, blocks - 1, lambda block: moments(block, 0))

    pl.semaphore_wait(barrier, qs - 1 + zs - 1)
    states_copy = copy(own_states, other_states, state_send, state_recv, (z, xy * 2 + other))
    states_copy.start()

    def gram_copy(o, *offset):
        to = target(*offset)
        return copy(gram_out.at[to[1]], gram_in.at[o], gram_send, gram_recv, to)

    around(2, lambda *at: gram_copy(*at).start())
    gram_in[0] = gram_out[q]
    moments(blocks - 1, 0)

    states_copy.wait_recv()
    prepare(other_states, 1)
    loop(0, blocks - 1, lambda block: moments(block, 1))

    wait_all(gram_in.at[1:qs], gram_send, gram_recv)
    gram_sum[...] = jnp.sum(gram_in[...], axis=0)

    def gall_copy(o, *offset):
        return copy(gram_sum, gram_all.at[q], gall_send, gall_recv, target(*offset))

    around(2, lambda *at: gall_copy(*at).start())
    gram_all[q] = gram_sum[...]
    moments(blocks - 1, 1)

    slot = core * slots + lax.broadcasted_iota(jnp.int32, (1, slots), 1)
    sets_ref[...] = jnp.where(slot < counts_ref[z], sets_ref[...], -1)
    notional = notionals_ref[...]
    notionals_ref[...] = jnp.where(notional > 0, 1.0, jnp.where(notional < 0, -1.0, 0.0))

    def owners(chunk):
        return pl.ds(chunk * per_chunk, per_chunk)

    def core_copy(chunk):
        return copy(
            net_ref.at[owners(chunk), other],
            core_in.at[owners(chunk)],
            core_send.at[chunk],
            core_recv.at[chunk],
            (z, xy * 2 + other),
        )

    def plane_copy(chunk, o, *offset):
        to = target(*offset)
        return copy(
            plane_out.at[owners(chunk), to[1] // 2],
            plane_in.at[o, owners(chunk)],
            plane_send.at[chunk],
            plane_recv.at[chunk],
            to,
        )

    def to_plane(chunk):
        core_copy(chunk).wait_recv()
        plane_out[owners(chunk)] = net_ref[owners(chunk), core] + core_in[owners(chunk)]
        around(1, lambda *at: plane_copy(chunk, *at).start())
        plane_in[0, owners(chunk)] = plane_out[owners(chunk), xy]

    def turn(i):
        return lax.rem(z // per_chunk + 1 + i, chunks)

    few = width * 3 // 16

    def more_steps(begin, count):
        loop(0, count // 4, lambda i: invert_steps(matrix_ref, begin + i * 4, 4))

    def net(i, first=False, begin=None):
        chunk = turn(i)
        row = lax.broadcasted_iota(jnp.int32, (set_count, slots), 0) + chunk * set_count
        member = jnp.where(row == sets_ref[...], notionals_ref[...], 0.0).astype(BF16)
        both = dot(member, moment_ref[...], 1, 1)
        if begin is not None:
            invert_steps(matrix_ref, begin, few)
        net_ref[owners(chunk)] = (both[:, :LANES] + both[:, LANES:]).reshape(per_chunk, *net_ref.shape[1:])
        core_copy(chunk).start()
        if not first:
            to_plane(turn(i - 1))

    net(0, True)
    loop(1, chunks - 2, net)
    wait_all(gram_all.at[1:qs], gall_send, gall_recv)
    for piece in range(qs):
        matrix_ref[piece * rows : (piece + 1) * rows, :] = gram_all[piece, 0:rows, :]
    loop(chunks - 2, chunks, lambda i: net(i, False, (i - chunks + 2) * few))
    to_plane(turn(chunks - 1))

    def z_copy(to):
        return copy(z_out.at[to], z_in.at[z], z_send, z_recv, (to, q))

    def others(act):
        def one(to):
            @pl.when(to != z)
            def _():
                act(to)

        return one

    def to_z(chunk):
        wait_all(plane_in.at[1:xys, owners(chunk)], plane_send.at[chunk], plane_recv.at[chunk])
        z_out[owners(chunk)] = jnp.sum(plane_in[:, owners(chunk)], axis=0)
        loop(chunk * per_chunk, (chunk + 1) * per_chunk, others(lambda to: z_copy(to).start()))

    loop(0, chunks - 2, lambda i: to_z(turn(i)))
    more_steps(2 * few, width - 4 * few)
    to_z(turn(chunks - 2))
    more_steps(width - 2 * few, few)
    to_z(turn(chunks - 1))
    z_in[z] = z_out[z]
    more_steps(width - few, few)
    inverse = matrix_ref[...]
    left = lax.broadcasted_iota(jnp.int32, inverse.shape, 1) < width
    block = jnp.concatenate([jnp.where(left, inverse, 0.0), jnp.where(left, 0.0, inverse)], axis=0)
    wait_all(z_in.at[1:zs], z_send, z_recv)
    own_ref[...] = dot(jnp.sum(z_in[...], axis=0), block, 1, 0, HIGHEST)

    mine = core * xys + xy

    def coeff_copy(o, *offset):
        return copy(own_ref, coeffs_ref.at[mine], coeff_send, coeff_recv, target(*offset))

    around(2, lambda *at: coeff_copy(*at).start())
    coeffs_ref[mine] = own_ref[...]
    sets = thresholds_ref.shape[1]
    limits = jnp.broadcast_to(0.25 * thresholds_ref[...].astype(F32), (LANES, sets)).T
    wait_all(coeffs_ref.at[1:qs], coeff_send, coeff_recv)

    high, low = split(coeffs_ref[...].reshape(sets, LANES))
    coeffs = jnp.concatenate([high, low, high], axis=1)
    weight = weight.astype(BF16)
    for date in range(dates):
        exposure = jnp.maximum(dot(coeffs, basis_ref[date], 1, 0) - limits[:, 0:1], 0.0)
        out_ref[date] = exposure
        high, low = split(exposure)
        part = dot(weight, high, 1, 1) + dot(weight, low, 1, 1)
        part_ref[q, date : date + 1, :] = part[0:1, :]

    def part_copy(o, *offset):
        return copy(part_ref.at[q], part_ref.at[q], part_send, part_recv, target(*offset))

    around(2, lambda *at: part_copy(*at).start())
    out_copy = pltpu.make_async_copy(out_ref, exposure_ref, out_sem)
    out_copy.start()
    states_copy.wait_send()
    sent_all(gram_in.at[1:qs], gram_send, gram_recv)
    sent_all(gram_all.at[1:qs], gall_send, gall_recv)
    loop(0, chunks, lambda chunk: core_copy(chunk).wait_send())
    loop(
        0, chunks, lambda chunk: sent_all(plane_in.at[1:xys, owners(chunk)], plane_send.at[chunk], plane_recv.at[chunk])
    )
    sent_all(z_in.at[1:zs], z_send, z_recv)
    sent_all(coeffs_ref.at[1:qs], coeff_send, coeff_recv)
    out_copy.wait()
    wait_all(part_ref.at[1:qs], part_send, part_recv)
    expected_ref[...] = jnp.sum(part_ref[...], axis=0) / gram_all[0, rows : rows + 1, 0:1]
    sent_all(part_ref.at[1:qs], part_send, part_recv)


def body(
    start_state, shocks, loadings, strikes, notionals, trade_set, live_counts, weights, thresholds
):
    zs, qs = lax.axis_size("trade"), lax.axis_size("path")
    xys = qs // 2
    paths, factors = start_state.shape
    dates = shocks.shape[0]
    width = 2 * factors
    slots = loadings.shape[1] // 2
    size = min(1024, slots)
    sets = thresholds.shape[0]
    per = sets // qs
    chunks = 4 if zs % 4 == 0 else zs
    tall = (width // qs + 8) // 8 * 8
    vmem = pl.BlockSpec(memory_space=pltpu.VMEM)
    hbm = pl.BlockSpec(memory_space=pl.ANY)
    dma = pltpu.SemaphoreType.DMA
    return pl.pallas_call(
        functools.partial(kernel, zs, xys, size),
        out_shape=(
            jax.ShapeDtypeStruct((dates, sets, paths), F32),
            jax.ShapeDtypeStruct((dates, sets), F32),
        ),
        in_specs=[hbm] * 4 + [pl.BlockSpec(memory_space=pltpu.SMEM)] + [hbm] * 4,
        out_specs=(hbm, vmem),
        scratch_shapes=[
            pltpu.VMEM((factors, paths), F32),
            pltpu.VMEM((dates, factors, paths), F32),
            pltpu.VMEM((1, paths), jnp.int32),
            pltpu.VMEM((1, sets), jnp.int32),
            pltpu.VMEM((factors, slots), F32),
            pltpu.VMEM((1, slots), F32),
            pltpu.VMEM((1, slots), F32),
            pltpu.VMEM((1, slots), jnp.int32),
            dma((8,)),
            pltpu.VMEM((dates, sets, paths), F32),
            dma,
            pltpu.VMEM(((dates + 1) * factors + 8, paths), F32),
            pltpu.VMEM(((dates + 1) * factors + 8, paths), F32),
            pltpu.VMEM((2, dates, paths, 4 * factors), BF16),
            pltpu.VMEM((2, dates, 2 * width, paths), BF16),
            pltpu.VMEM((dates, 3 * dates * width, paths), BF16),
            pltpu.VMEM((LANES, slots), F32),
            pltpu.VMEM((2 * LANES, slots), BF16),
            pltpu.VMEM((qs, tall, LANES), F32),
            pltpu.VMEM((qs, tall, LANES), F32),
            pltpu.VMEM((tall, LANES), F32),
            pltpu.VMEM((qs, tall, LANES), F32),
            pltpu.VMEM((width, LANES), F32),
            pltpu.VMEM((zs, 2, xys, per, LANES), F32),
            pltpu.VMEM((zs, xys, per, LANES), F32),
            pltpu.VMEM((zs, xys, per, LANES), F32),
            pltpu.VMEM((xys, zs, per, LANES), F32),
            pltpu.VMEM((zs, per, LANES), F32),
            pltpu.VMEM((zs, per, LANES), F32),
            pltpu.VMEM((per, LANES), F32),
            pltpu.VMEM((qs, per, LANES), F32),
            pltpu.VMEM((qs, dates, sets), F32),
            dma, dma, dma, dma, dma, dma, dma((chunks,)), dma((chunks,)), dma((chunks,)), dma((chunks,)),
            dma, dma, dma, dma, dma, dma,
        ],
        compiler_params=pltpu.CompilerParams(
            collective_id=0, has_side_effects=True, vmem_limit_bytes=56 << 20
        ),
        name="exposures",
    )(
        start_state.T, shocks.transpose(0, 2, 1), weights.reshape(1, -1), thresholds.reshape(1, -1), live_counts,
        loadings, strikes.reshape(1, -1), notionals.reshape(1, -1), trade_set.reshape(1, -1),
    )


def solution(mesh):
    placed = (
        P("path", None),
        P(None, "path", None),
        P(None, "trade"),
        P("trade"),
        P("trade"),
        P("trade"),
        P(),
        P("path"),
        P("trade"),
    )
    return jax.shard_map(
        body,
        mesh=mesh,
        in_specs=placed,
        out_specs=(P(None, "trade", "path"), P(None, "trade")),
        check_vma=False,
    )
```

```python
import functools

import jax
import jax.numpy as jnp
from jax import lax
from jax.experimental import pallas as pl
from jax.experimental.pallas import tpu as pltpu
from jax.sharding import PartitionSpec as P

ROOT_HALF = 0.7071067811865476
F32, BF16 = jnp.float32, jnp.bfloat16
HIGHEST = lax.Precision.HIGHEST
MESH = pl.DeviceIdType.MESH
LANES = 128


def split(value):
    high = value.astype(BF16)
    return high, (value - high.astype(F32)).astype(BF16)


def dot(left, right, left_dim, right_dim, precision=None):
    return lax.dot_general(
        left, right, (((left_dim,), (right_dim,)), ((), ())), precision=precision, preferred_element_type=F32
    )


def make_basis(state):
    return jnp.concatenate([state, (state * state - 1.0) * ROOT_HALF], axis=0)


def scaled_trades(loadings_ref, strikes_ref, notionals_ref, block, size):
    cols = pl.ds(pl.multiple_of(block * size, size), size)
    scale = jnp.abs(notionals_ref[:, cols])
    high, low = split(loadings_ref[:, cols] * scale)
    strike = strikes_ref[:, cols] * (-scale)
    first = strike.astype(BF16).astype(F32)
    second = (strike - first).astype(BF16).astype(F32)
    third = (strike - first) - second
    row = lax.broadcasted_iota(jnp.int32, high.shape, 0)
    parts = jnp.where(row == 0, first, jnp.where(row == 1, second, jnp.where(row == 2, third, 0.0)))
    return jnp.concatenate([high, low, high, parts.astype(BF16)], axis=0)


def invert_steps(matrix_ref, begin, count):
    size = matrix_ref.shape[0]
    lane = lax.broadcasted_iota(jnp.int32, (size, LANES), 1)
    row_id = lax.broadcasted_iota(jnp.int32, (size, LANES), 0)
    lane_row = lax.broadcasted_iota(jnp.int32, (1, LANES), 1)

    for j in [begin + i for i in range(count)]:
        matrix = matrix_ref[...]
        row = matrix_ref[pl.ds(j, 1), :]

        def pick(entries, ids, j=j):
            first = jnp.sum(jnp.where(ids == j, entries, 0.0), axis=1, keepdims=True)
            second = jnp.sum(jnp.where(ids == j + size, entries, 0.0), axis=1, keepdims=True)
            return jnp.where(ids < size, first, second)

        column = pick(matrix, lane)
        inverse = 1.0 / pick(row, lane_row)
        scaled = row * inverse
        here = jnp.logical_or(lane == j, lane == j + size)
        reduced = jnp.where(here, -column * inverse, matrix - column * scaled)
        pivot_row = jnp.where(jnp.logical_or(lane_row == j, lane_row == j + size), inverse, scaled)
        matrix_ref[...] = jnp.where(row_id == j, pivot_row, reduced)


def loop(begin, end, act):
    def step(i, carry):
        act(i)
        return carry

    lax.fori_loop(begin, end, step, 0)


def kernel(
    zs, xys, size,
    start_hbm, shocks_hbm, weights_hbm, thresholds_hbm, counts_ref, loadings_hbm, strikes_hbm, notionals_hbm, sets_hbm,
    exposure_ref, expected_ref,
    start_ref, shocks_ref, weights_ref, thresholds_ref,
    loadings_ref, strikes_ref, notionals_ref, sets_ref, local_sem, out_ref, out_sem,
    own_states, other_states, state_ref, wbasis_ref, basis_ref, total_ref, moment_ref,
    gram_out, gram_in, gram_sum, gram_all, matrix_ref,
    net_ref, core_in, plane_out, plane_in, z_out, z_in, own_ref, coeffs_ref, part_ref,
    state_send, state_recv, gram_send, gram_recv, gall_send, gall_recv, core_send, core_recv, plane_send, plane_recv,
    z_send, z_recv, coeff_send, coeff_recv, part_send, part_recv,
):
    z = lax.axis_index("trade")
    q = lax.axis_index("path")
    xy, core = q // 2, lax.rem(q, 2)
    other = 1 - core
    qs = 2 * xys
    factors, paths = start_ref.shape
    dates = shocks_ref.shape[0]
    width = 2 * factors
    slots = loadings_ref.shape[1]
    chunks = core_send.shape[0]
    per_chunk = zs // chunks
    set_count = per_chunk * thresholds_ref.shape[1]

    def copy(src, dst, send, recv, device):
        return pltpu.make_async_remote_copy(
            src_ref=src, dst_ref=dst, send_sem=send, recv_sem=recv, device_id=device, device_id_type=MESH
        )

    def target(cores, o):
        return (z, lax.rem(q + o, qs) if cores == 2 else lax.rem(xy + o, xys) * 2 + core)

    def wait_all(ref, send, recv):
        copy(ref, ref, send, recv, target(2, 1)).wait_recv()

    def sent_all(ref, send, recv):
        copy(ref, ref, send, recv, target(2, 1)).wait_send()

    def around(cores, act):
        loop(1, cores * xys, lambda o: act(o, cores, o))

    half = pl.ds(pl.multiple_of(core * slots, slots), slots)
    fetches = [
        pltpu.make_async_copy(hbm.at[:, half], ref, local_sem.at[i])
        for i, (hbm, ref) in enumerate(
            [
                (loadings_hbm, loadings_ref),
                (strikes_hbm, strikes_ref),
                (notionals_hbm, notionals_ref),
                (sets_hbm, sets_ref),
            ]
        )
    ]
    firsts = [
        pltpu.make_async_copy(hbm, ref, local_sem.at[len(fetches) + i])
        for i, (hbm, ref) in enumerate(
            [
                (start_hbm, start_ref),
                (shocks_hbm, shocks_ref),
                (weights_hbm, weights_ref),
                (thresholds_hbm, thresholds_ref),
            ]
        )
    ]
    for fetch in firsts + fetches:
        fetch.start()

    barrier = pltpu.get_barrier_semaphore()

    def greet(device):
        pl.semaphore_signal(barrier, inc=1, device_id=device, device_id_type=MESH)

    loop(1, qs, lambda o: greet((z, lax.rem(q + o, qs))))
    loop(1, zs, lambda o: greet((lax.rem(z + o, zs), q)))

    for fetch in firsts:
        fetch.wait()
    weight = jnp.broadcast_to(weights_ref[...].astype(F32), (8, paths))
    state = start_ref[...]
    own_states[0:factors, :] = state
    for date in range(dates):
        state = 0.8 * state + 0.6 * shocks_ref[date]
        own_states[(date + 1) * factors : (date + 2) * factors, :] = state
    bottom = (dates + 1) * factors
    own_states[bottom : bottom + 8, :] = weight

    def prepare(states, place):
        scale = states[bottom : bottom + 1, :]
        grams = []
        for date in range(dates):
            basis = make_basis(states[date * factors : (date + 1) * factors, :])
            weighted = basis * scale
            high, low = split(weighted)
            wbasis_ref[place, date, 0:width, :] = high
            wbasis_ref[place, date, width : 2 * width, :] = low
            future = states[(date + 1) * factors : (date + 2) * factors, :]
            high = future.astype(BF16).astype(F32)
            ones = jnp.where(lax.broadcasted_iota(jnp.int32, future.shape, 0) < 3, 1.0, 0.0)
            rows = jnp.concatenate([high, high, future - high, ones], axis=0)
            state_ref[place, date] = rows.T.astype(BF16)
            if place == 0:
                grams.append(dot(weighted, basis, 1, 1, HIGHEST))
                high, low = split(basis)
                zero = jnp.zeros_like(high)
                for part, entries in enumerate((high, high, low)):
                    for k in range(dates):
                        at = part * dates * width + k * width
                        basis_ref[date, at : at + width, :] = entries if k == date else zero
        return grams

    def moments(block, place):
        trades = scaled_trades(loadings_ref, strikes_ref, notionals_ref, block, size)
        cols = pl.ds(pl.multiple_of(block * size, size), size)
        for date in range(dates):
            flows = jnp.maximum(dot(state_ref[place, date], trades, 1, 0), 0.0)
            high, low = split(flows)
            both = dot(wbasis_ref[place, date], high, 1, 0)
            least = dot(wbasis_ref[place, date, 0:width, :], low, 1, 0)
            moment = both[0:width] + both[width:] + least
            at = date * width
            if place == 0:
                total_ref[at : at + width, cols] = moment
            else:
                high, low = split(moment + total_ref[at : at + width, cols])
                moment_ref[at : at + width, cols] = high
                moment_ref[LANES + at : LANES + at + width, cols] = low

    gram = jnp.concatenate(prepare(own_states, 0), axis=1)
    rows = width // qs
    for piece in range(qs):
        gram_out[piece, 0:rows, :] = gram[piece * rows : (piece + 1) * rows, :]
        gram_out[piece, rows : rows + 1, :] = jnp.broadcast_to(jnp.sum(weight[0:1, :], axis=1, keepdims=True), (1, LANES))
    for fetch in fetches:
        fetch.wait()
    blocks = slots // size
    loop(0, blocks - 1, lambda block: moments(block, 0))

    pl.semaphore_wait(barrier, qs - 1 + zs - 1)
    states_copy = copy(own_states, other_states, state_send, state_recv, (z, xy * 2 + other))
    states_copy.start()

    def gram_copy(o, *offset):
        to = target(*offset)
        return copy(gram_out.at[to[1]], gram_in.at[o], gram_send, gram_recv, to)

    around(2, lambda *at: gram_copy(*at).start())
    gram_in[0] = gram_out[q]
    moments(blocks - 1, 0)

    states_copy.wait_recv()
    prepare(other_states, 1)
    loop(0, blocks - 1, lambda block: moments(block, 1))

    wait_all(gram_in.at[1:qs], gram_send, gram_recv)
    gram_sum[...] = jnp.sum(gram_in[...], axis=0)

    def gall_copy(o, *offset):
        return copy(gram_sum, gram_all.at[q], gall_send, gall_recv, target(*offset))

    around(2, lambda *at: gall_copy(*at).start())
    gram_all[q] = gram_sum[...]
    moments(blocks - 1, 1)

    slot = core * slots + lax.broadcasted_iota(jnp.int32, (1, slots), 1)
    sets_ref[...] = jnp.where(slot < counts_ref[z], sets_ref[...], -1)
    notional = notionals_ref[...]
    notionals_ref[...] = jnp.where(notional > 0, 1.0, jnp.where(notional < 0, -1.0, 0.0))

    def owners(chunk):
        return pl.ds(chunk * per_chunk, per_chunk)

    def core_copy(chunk):
        return copy(
            net_ref.at[owners(chunk), other],
            core_in.at[owners(chunk)],
            core_send.at[chunk],
            core_recv.at[chunk],
            (z, xy * 2 + other),
        )

    def plane_copy(chunk, o, *offset):
        to = target(*offset)
        return copy(
            plane_out.at[owners(chunk), to[1] // 2],
            plane_in.at[o, owners(chunk)],
            plane_send.at[chunk],
            plane_recv.at[chunk],
            to,
        )

    def to_plane(chunk):
        core_copy(chunk).wait_recv()
        plane_out[owners(chunk)] = net_ref[owners(chunk), core] + core_in[owners(chunk)]
        around(1, lambda *at: plane_copy(chunk, *at).start())
        plane_in[0, owners(chunk)] = plane_out[owners(chunk), xy]

    def turn(i):
        return lax.rem(z // per_chunk + 1 + i, chunks)

    few = width * 3 // 16
    late = chunks // 2
    beside = 2 * few // late

    def more_steps(begin, count):
        loop(0, count // 4, lambda i: invert_steps(matrix_ref, begin + i * 4, 4))

    def net(i, first=False, begin=None):
        chunk = turn(i)
        row = lax.broadcasted_iota(jnp.int32, (set_count, slots), 0) + chunk * set_count
        member = jnp.where(row == sets_ref[...], notionals_ref[...], 0.0).astype(BF16)
        both = dot(member, moment_ref[...], 1, 1)
        if begin is not None:
            invert_steps(matrix_ref, begin, beside)
        net_ref[owners(chunk)] = (both[:, :LANES] + both[:, LANES:]).reshape(per_chunk, *net_ref.shape[1:])
        core_copy(chunk).start()
        if not first:
            to_plane(turn(i - 1))

    net(0, True)
    loop(1, chunks - late, net)
    wait_all(gram_all.at[1:qs], gall_send, gall_recv)
    for piece in range(qs):
        matrix_ref[piece * rows : (piece + 1) * rows, :] = gram_all[piece, 0:rows, :]
    loop(chunks - late, chunks, lambda i: net(i, False, (i - chunks + late) * beside))
    to_plane(turn(chunks - 1))

    def z_copy(to):
        return copy(z_out.at[to], z_in.at[z], z_send, z_recv, (to, q))

    def others(act):
        def one(to):
            @pl.when(to != z)
            def _():
                act(to)

        return one

    def to_z(chunk):
        wait_all(plane_in.at[1:xys, owners(chunk)], plane_send.at[chunk], plane_recv.at[chunk])
        z_out[owners(chunk)] = jnp.sum(plane_in[:, owners(chunk)], axis=0)
        loop(chunk * per_chunk, (chunk + 1) * per_chunk, others(lambda to: z_copy(to).start()))

    loop(0, chunks - 2, lambda i: to_z(turn(i)))
    more_steps(2 * few, width - 4 * few)
    to_z(turn(chunks - 2))
    more_steps(width - 2 * few, few)
    to_z(turn(chunks - 1))
    z_in[z] = z_out[z]
    more_steps(width - few, few)
    inverse = matrix_ref[...]
    left = lax.broadcasted_iota(jnp.int32, inverse.shape, 1) < width
    block = jnp.concatenate([jnp.where(left, inverse, 0.0), jnp.where(left, 0.0, inverse)], axis=0)
    wait_all(z_in.at[1:zs], z_send, z_recv)
    own_ref[...] = dot(jnp.sum(z_in[...], axis=0), block, 1, 0, HIGHEST)

    mine = core * xys + xy

    def coeff_copy(o, *offset):
        return copy(own_ref, coeffs_ref.at[mine], coeff_send, coeff_recv, target(*offset))

    around(2, lambda *at: coeff_copy(*at).start())
    coeffs_ref[mine] = own_ref[...]
    sets = thresholds_ref.shape[1]
    limits = jnp.broadcast_to(0.25 * thresholds_ref[...].astype(F32), (LANES, sets)).T
    wait_all(coeffs_ref.at[1:qs], coeff_send, coeff_recv)

    high, low = split(coeffs_ref[...].reshape(sets, LANES))
    coeffs = jnp.concatenate([high, low, high], axis=1)
    weight = weight.astype(BF16)
    for date in range(dates):
        exposure = jnp.maximum(dot(coeffs, basis_ref[date], 1, 0) - limits[:, 0:1], 0.0)
        out_ref[date] = exposure
        high, low = split(exposure)
        part = dot(weight, high, 1, 1) + dot(weight, low, 1, 1)
        part_ref[q, date : date + 1, :] = part[0:1, :]

    def part_copy(o, *offset):
        return copy(part_ref.at[q], part_ref.at[q], part_send, part_recv, target(*offset))

    around(2, lambda *at: part_copy(*at).start())
    out_copy = pltpu.make_async_copy(out_ref, exposure_ref, out_sem)
    out_copy.start()
    states_copy.wait_send()
    sent_all(gram_in.at[1:qs], gram_send, gram_recv)
    sent_all(gram_all.at[1:qs], gall_send, gall_recv)
    loop(0, chunks, lambda chunk: core_copy(chunk).wait_send())
    loop(
        0, chunks, lambda chunk: sent_all(plane_in.at[1:xys, owners(chunk)], plane_send.at[chunk], plane_recv.at[chunk])
    )
    sent_all(z_in.at[1:zs], z_send, z_recv)
    sent_all(coeffs_ref.at[1:qs], coeff_send, coeff_recv)
    out_copy.wait()
    wait_all(part_ref.at[1:qs], part_send, part_recv)
    expected_ref[...] = jnp.sum(part_ref[...], axis=0) / gram_all[0, rows : rows + 1, 0:1]
    sent_all(part_ref.at[1:qs], part_send, part_recv)


def body(
    start_state, shocks, loadings, strikes, notionals, trade_set, live_counts, weights, thresholds
):
    zs, qs = lax.axis_size("trade"), lax.axis_size("path")
    xys = qs // 2
    paths, factors = start_state.shape
    dates = shocks.shape[0]
    width = 2 * factors
    slots = loadings.shape[1] // 2
    size = min(1024, slots)
    sets = thresholds.shape[0]
    per = sets // qs
    chunks = zs
    tall = (width // qs + 8) // 8 * 8
    vmem = pl.BlockSpec(memory_space=pltpu.VMEM)
    hbm = pl.BlockSpec(memory_space=pl.ANY)
    dma = pltpu.SemaphoreType.DMA
    return pl.pallas_call(
        functools.partial(kernel, zs, xys, size),
        out_shape=(
            jax.ShapeDtypeStruct((dates, sets, paths), F32),
            jax.ShapeDtypeStruct((dates, sets), F32),
        ),
        in_specs=[hbm] * 4 + [pl.BlockSpec(memory_space=pltpu.SMEM)] + [hbm] * 4,
        out_specs=(hbm, vmem),
        scratch_shapes=[
            pltpu.VMEM((factors, paths), F32),
            pltpu.VMEM((dates, factors, paths), F32),
            pltpu.VMEM((1, paths), jnp.int32),
            pltpu.VMEM((1, sets), jnp.int32),
            pltpu.VMEM((factors, slots), F32),
            pltpu.VMEM((1, slots), F32),
            pltpu.VMEM((1, slots), F32),
            pltpu.VMEM((1, slots), jnp.int32),
            dma((8,)),
            pltpu.VMEM((dates, sets, paths), F32),
            dma,
            pltpu.VMEM(((dates + 1) * factors + 8, paths), F32),
            pltpu.VMEM(((dates + 1) * factors + 8, paths), F32),
            pltpu.VMEM((2, dates, paths, 4 * factors), BF16),
            pltpu.VMEM((2, dates, 2 * width, paths), BF16),
            pltpu.VMEM((dates, 3 * dates * width, paths), BF16),
            pltpu.VMEM((LANES, slots), F32),
            pltpu.VMEM((2 * LANES, slots), BF16),
            pltpu.VMEM((qs, tall, LANES), F32),
            pltpu.VMEM((qs, tall, LANES), F32),
            pltpu.VMEM((tall, LANES), F32),
            pltpu.VMEM((qs, tall, LANES), F32),
            pltpu.VMEM((width, LANES), F32),
            pltpu.VMEM((zs, 2, xys, per, LANES), F32),
            pltpu.VMEM((zs, xys, per, LANES), F32),
            pltpu.VMEM((zs, xys, per, LANES), F32),
            pltpu.VMEM((xys, zs, per, LANES), F32),
            pltpu.VMEM((zs, per, LANES), F32),
            pltpu.VMEM((zs, per, LANES), F32),
            pltpu.VMEM((per, LANES), F32),
            pltpu.VMEM((qs, per, LANES), F32),
            pltpu.VMEM((qs, dates, sets), F32),
            dma, dma, dma, dma, dma, dma, dma((chunks,)), dma((chunks,)), dma((chunks,)), dma((chunks,)),
            dma, dma, dma, dma, dma, dma,
        ],
        compiler_params=pltpu.CompilerParams(
            collective_id=0, has_side_effects=True, vmem_limit_bytes=56 << 20
        ),
        name="exposures",
    )(
        start_state.T, shocks.transpose(0, 2, 1), weights.reshape(1, -1), thresholds.reshape(1, -1), live_counts,
        loadings, strikes.reshape(1, -1), notionals.reshape(1, -1), trade_set.reshape(1, -1),
    )


def solution(mesh):
    placed = (
        P("path", None),
        P(None, "path", None),
        P(None, "trade"),
        P("trade"),
        P("trade"),
        P("trade"),
        P(),
        P("path"),
        P("trade"),
    )
    return jax.shard_map(
        body,
        mesh=mesh,
        in_specs=placed,
        out_specs=(P(None, "trade", "path"), P(None, "trade")),
        check_vma=False,
    )
```

```python
import functools

import jax
import jax.numpy as jnp
from jax import lax
from jax.experimental import pallas as pl
from jax.experimental.pallas import tpu as pltpu
from jax.sharding import PartitionSpec as P

ROOT_HALF = 0.7071067811865476
F32, BF16 = jnp.float32, jnp.bfloat16
HIGHEST = lax.Precision.HIGHEST
MESH = pl.DeviceIdType.MESH
LANES = 128


def split(value):
    high = value.astype(BF16)
    return high, (value - high.astype(F32)).astype(BF16)


def dot(left, right, left_dim, right_dim, precision=None):
    return lax.dot_general(
        left, right, (((left_dim,), (right_dim,)), ((), ())), precision=precision, preferred_element_type=F32
    )


def make_basis(state):
    return jnp.concatenate([state, (state * state - 1.0) * ROOT_HALF], axis=0)


def scaled_trades(loadings_ref, strikes_ref, notionals_ref, block, size):
    cols = pl.ds(pl.multiple_of(block * size, size), size)
    scale = jnp.abs(notionals_ref[:, cols])
    high, low = split(loadings_ref[:, cols] * scale)
    strike = strikes_ref[:, cols] * (-scale)
    first = strike.astype(BF16).astype(F32)
    second = (strike - first).astype(BF16).astype(F32)
    third = (strike - first) - second
    row = lax.broadcasted_iota(jnp.int32, high.shape, 0)
    parts = jnp.where(row == 0, first, jnp.where(row == 1, second, jnp.where(row == 2, third, 0.0)))
    return jnp.concatenate([high, low, high, parts.astype(BF16)], axis=0)


def invert_steps(matrix_ref, begin, count):
    size = matrix_ref.shape[0]
    lane = lax.broadcasted_iota(jnp.int32, (size, LANES), 1)
    row_id = lax.broadcasted_iota(jnp.int32, (size, LANES), 0)
    lane_row = lax.broadcasted_iota(jnp.int32, (1, LANES), 1)

    for j in [begin + i for i in range(count)]:
        matrix = matrix_ref[...]
        row = matrix_ref[pl.ds(j, 1), :]

        def pick(entries, ids, j=j):
            first = jnp.sum(jnp.where(ids == j, entries, 0.0), axis=1, keepdims=True)
            second = jnp.sum(jnp.where(ids == j + size, entries, 0.0), axis=1, keepdims=True)
            return jnp.where(ids < size, first, second)

        column = pick(matrix, lane)
        inverse = 1.0 / pick(row, lane_row)
        scaled = row * inverse
        here = jnp.logical_or(lane == j, lane == j + size)
        reduced = jnp.where(here, -column * inverse, matrix - column * scaled)
        pivot_row = jnp.where(jnp.logical_or(lane_row == j, lane_row == j + size), inverse, scaled)
        matrix_ref[...] = jnp.where(row_id == j, pivot_row, reduced)


def loop(begin, end, act):
    def step(i, carry):
        act(i)
        return carry

    lax.fori_loop(begin, end, step, 0)


def kernel(
    zs, xys, size,
    start_hbm, shocks_hbm, weights_hbm, thresholds_hbm, counts_ref, loadings_hbm, strikes_hbm, notionals_hbm, sets_hbm,
    result_ref, expected_ref,
    start_ref, shocks_ref, weights_ref, thresholds_ref,
    loadings_ref, strikes_ref, notionals_ref, sets_ref, local_sem,
    own_states, other_states, state_ref, wbasis_ref, basis_ref, total_ref, moment_ref,
    gram_out, gram_in, gram_sum, gram_all, matrix_ref,
    net_ref, core_in, plane_out, plane_in, z_out, z_in, own_ref, coeffs_ref, part_ref,
    state_send, state_recv, gram_send, gram_recv, gall_send, gall_recv, core_send, core_recv, plane_send, plane_recv,
    z_send, z_recv, coeff_send, coeff_recv, part_send, part_recv,
):
    z = lax.axis_index("trade")
    q = lax.axis_index("path")
    xy, core = q // 2, lax.rem(q, 2)
    other = 1 - core
    qs = 2 * xys
    factors, paths = start_ref.shape
    dates = shocks_ref.shape[0]
    width = 2 * factors
    slots = loadings_ref.shape[1]
    chunks = core_send.shape[0]
    per_chunk = zs // chunks
    set_count = per_chunk * thresholds_ref.shape[1]

    def copy(src, dst, send, recv, device):
        return pltpu.make_async_remote_copy(
            src_ref=src, dst_ref=dst, send_sem=send, recv_sem=recv, device_id=device, device_id_type=MESH
        )

    def target(cores, o):
        return (z, lax.rem(q + o, qs) if cores == 2 else lax.rem(xy + o, xys) * 2 + core)

    def wait_all(ref, send, recv):
        copy(ref, ref, send, recv, target(2, 1)).wait_recv()

    def sent_all(ref, send, recv):
        copy(ref, ref, send, recv, target(2, 1)).wait_send()

    def around(cores, act):
        loop(1, cores * xys, lambda o: act(o, cores, o))

    half = pl.ds(pl.multiple_of(core * slots, slots), slots)
    fetches = [
        pltpu.make_async_copy(hbm.at[:, half], ref, local_sem.at[i])
        for i, (hbm, ref) in enumerate(
            [
                (loadings_hbm, loadings_ref),
                (strikes_hbm, strikes_ref),
                (notionals_hbm, notionals_ref),
                (sets_hbm, sets_ref),
            ]
        )
    ]
    firsts = [
        pltpu.make_async_copy(hbm, ref, local_sem.at[len(fetches) + i])
        for i, (hbm, ref) in enumerate(
            [
                (start_hbm, start_ref),
                (shocks_hbm, shocks_ref),
                (weights_hbm, weights_ref),
                (thresholds_hbm, thresholds_ref),
            ]
        )
    ]
    for fetch in firsts + fetches:
        fetch.start()

    barrier = pltpu.get_barrier_semaphore()

    def greet(device):
        pl.semaphore_signal(barrier, inc=1, device_id=device, device_id_type=MESH)

    loop(1, qs, lambda o: greet((z, lax.rem(q + o, qs))))
    loop(1, zs, lambda o: greet((lax.rem(z + o, zs), q)))

    for fetch in firsts:
        fetch.wait()
    weight = jnp.broadcast_to(weights_ref[...].astype(F32), (8, paths))
    state = start_ref[...]
    own_states[0:factors, :] = state
    for date in range(dates):
        state = 0.8 * state + 0.6 * shocks_ref[date]
        own_states[(date + 1) * factors : (date + 2) * factors, :] = state
    bottom = (dates + 1) * factors
    own_states[bottom : bottom + 8, :] = weight

    def prepare(states, place):
        scale = states[bottom : bottom + 1, :]
        grams = []
        for date in range(dates):
            basis = make_basis(states[date * factors : (date + 1) * factors, :])
            weighted = basis * scale
            high, low = split(weighted)
            wbasis_ref[place, date, 0:width, :] = high
            wbasis_ref[place, date, width : 2 * width, :] = low
            future = states[(date + 1) * factors : (date + 2) * factors, :]
            high = future.astype(BF16).astype(F32)
            ones = jnp.where(lax.broadcasted_iota(jnp.int32, future.shape, 0) < 3, 1.0, 0.0)
            rows = jnp.concatenate([high, high, future - high, ones], axis=0)
            state_ref[place, date] = rows.T.astype(BF16)
            if place == 0:
                grams.append(dot(weighted, basis, 1, 1, HIGHEST))
                high, low = split(basis)
                zero = jnp.zeros_like(high)
                for part, entries in enumerate((high, high, low)):
                    for k in range(dates):
                        at = part * dates * width + k * width
                        basis_ref[date, at : at + width, :] = entries if k == date else zero
        return grams

    def moments(block, place):
        trades = scaled_trades(loadings_ref, strikes_ref, notionals_ref, block, size)
        cols = pl.ds(pl.multiple_of(block * size, size), size)
        for date in range(dates):
            flows = jnp.maximum(dot(state_ref[place, date], trades, 1, 0), 0.0)
            high, low = split(flows)
            both = dot(wbasis_ref[place, date], high, 1, 0)
            least = dot(wbasis_ref[place, date, 0:width, :], low, 1, 0)
            moment = both[0:width] + both[width:] + least
            at = date * width
            if place == 0:
                total_ref[at : at + width, cols] = moment
            else:
                high, low = split(moment + total_ref[at : at + width, cols])
                moment_ref[at : at + width, cols] = high
                moment_ref[LANES + at : LANES + at + width, cols] = low

    gram = jnp.concatenate(prepare(own_states, 0), axis=1)
    rows = width // qs
    for piece in range(qs):
        gram_out[piece, 0:rows, :] = gram[piece * rows : (piece + 1) * rows, :]
        gram_out[piece, rows : rows + 1, :] = jnp.broadcast_to(jnp.sum(weight[0:1, :], axis=1, keepdims=True), (1, LANES))
    for fetch in fetches:
        fetch.wait()
    blocks = slots // size
    loop(0, blocks - 1, lambda block: moments(block, 0))

    pl.semaphore_wait(barrier, qs - 1 + zs - 1)
    states_copy = copy(own_states, other_states, state_send, state_recv, (z, xy * 2 + other))
    states_copy.start()

    def gram_copy(o, *offset):
        to = target(*offset)
        return copy(gram_out.at[to[1]], gram_in.at[o], gram_send, gram_recv, to)

    around(2, lambda *at: gram_copy(*at).start())
    gram_in[0] = gram_out[q]
    moments(blocks - 1, 0)

    states_copy.wait_recv()
    prepare(other_states, 1)
    loop(0, blocks - 1, lambda block: moments(block, 1))

    wait_all(gram_in.at[1:qs], gram_send, gram_recv)
    gram_sum[...] = jnp.sum(gram_in[...], axis=0)

    def gall_copy(o, *offset):
        return copy(gram_sum, gram_all.at[q], gall_send, gall_recv, target(*offset))

    around(2, lambda *at: gall_copy(*at).start())
    gram_all[q] = gram_sum[...]
    moments(blocks - 1, 1)

    slot = core * slots + lax.broadcasted_iota(jnp.int32, (1, slots), 1)
    sets_ref[...] = jnp.where(slot < counts_ref[z], sets_ref[...], -1)
    notional = notionals_ref[...]
    notionals_ref[...] = jnp.where(notional > 0, 1.0, jnp.where(notional < 0, -1.0, 0.0))

    def owners(chunk):
        return pl.ds(chunk * per_chunk, per_chunk)

    def core_copy(chunk):
        return copy(
            net_ref.at[owners(chunk), other],
            core_in.at[owners(chunk)],
            core_send.at[chunk],
            core_recv.at[chunk],
            (z, xy * 2 + other),
        )

    def plane_copy(chunk, o, *offset):
        to = target(*offset)
        return copy(
            plane_out.at[owners(chunk), to[1] // 2],
            plane_in.at[o, owners(chunk)],
            plane_send.at[chunk],
            plane_recv.at[chunk],
            to,
        )

    def to_plane(chunk):
        core_copy(chunk).wait_recv()
        plane_out[owners(chunk)] = net_ref[owners(chunk), core] + core_in[owners(chunk)]
        around(1, lambda *at: plane_copy(chunk, *at).start())
        plane_in[0, owners(chunk)] = plane_out[owners(chunk), xy]

    def turn(i):
        return lax.rem(z // per_chunk + 1 + i, chunks)

    few = width * 3 // 16
    late = chunks // 2
    beside = 2 * few // late

    def more_steps(begin, count):
        loop(0, count // 4, lambda i: invert_steps(matrix_ref, begin + i * 4, 4))

    def net(i, first=False, begin=None):
        chunk = turn(i)
        row = lax.broadcasted_iota(jnp.int32, (set_count, slots), 0) + chunk * set_count
        member = jnp.where(row == sets_ref[...], notionals_ref[...], 0.0).astype(BF16)
        both = dot(member, moment_ref[...], 1, 1)
        if begin is not None:
            invert_steps(matrix_ref, begin, beside)
        net_ref[owners(chunk)] = (both[:, :LANES] + both[:, LANES:]).reshape(per_chunk, *net_ref.shape[1:])
        core_copy(chunk).start()
        if not first:
            to_plane(turn(i - 1))

    net(0, True)
    loop(1, chunks - late, net)
    wait_all(gram_all.at[1:qs], gall_send, gall_recv)
    for piece in range(qs):
        matrix_ref[piece * rows : (piece + 1) * rows, :] = gram_all[piece, 0:rows, :]
    loop(chunks - late, chunks, lambda i: net(i, False, (i - chunks + late) * beside))
    to_plane(turn(chunks - 1))

    def z_copy(to):
        return copy(z_out.at[to], z_in.at[z], z_send, z_recv, (to, q))

    def others(act):
        def one(to):
            @pl.when(to != z)
            def _():
                act(to)

        return one

    def to_z(chunk):
        wait_all(plane_in.at[1:xys, owners(chunk)], plane_send.at[chunk], plane_recv.at[chunk])
        z_out[owners(chunk)] = jnp.sum(plane_in[:, owners(chunk)], axis=0)
        loop(chunk * per_chunk, (chunk + 1) * per_chunk, others(lambda to: z_copy(to).start()))

    loop(0, chunks - 2, lambda i: to_z(turn(i)))
    more_steps(2 * few, width - 4 * few)
    to_z(turn(chunks - 2))
    more_steps(width - 2 * few, few)
    to_z(turn(chunks - 1))
    z_in[z] = z_out[z]
    more_steps(width - few, few)
    inverse = matrix_ref[...]
    left = lax.broadcasted_iota(jnp.int32, inverse.shape, 1) < width
    block = jnp.concatenate([jnp.where(left, inverse, 0.0), jnp.where(left, 0.0, inverse)], axis=0)
    wait_all(z_in.at[1:zs], z_send, z_recv)
    own_ref[...] = dot(jnp.sum(z_in[...], axis=0), block, 1, 0, HIGHEST)

    mine = core * xys + xy

    def coeff_copy(o, *offset):
        return copy(own_ref, coeffs_ref.at[mine], coeff_send, coeff_recv, target(*offset))

    around(2, lambda *at: coeff_copy(*at).start())
    coeffs_ref[mine] = own_ref[...]
    sets = thresholds_ref.shape[1]
    limits = jnp.broadcast_to(0.25 * thresholds_ref[...].astype(F32), (LANES, sets)).T
    wait_all(coeffs_ref.at[1:qs], coeff_send, coeff_recv)

    high, low = split(coeffs_ref[...].reshape(sets, LANES))
    coeffs = jnp.concatenate([high, low, high], axis=1)
    weight = weight.astype(BF16)
    for date in range(dates):
        exposure = jnp.maximum(dot(coeffs, basis_ref[date], 1, 0) - limits[:, 0:1], 0.0)
        high, low = split(exposure)
        part = dot(weight, high, 1, 1) + dot(weight, low, 1, 1)
        part_ref[q, date : date + 1, :] = part[0:1, :]

    def part_copy(o, *offset):
        return copy(part_ref.at[q], part_ref.at[q], part_send, part_recv, target(*offset))

    around(2, lambda *at: part_copy(*at).start())
    result_ref[...] = coeffs_ref[...]
    states_copy.wait_send()
    sent_all(gram_in.at[1:qs], gram_send, gram_recv)
    sent_all(gram_all.at[1:qs], gall_send, gall_recv)
    loop(0, chunks, lambda chunk: core_copy(chunk).wait_send())
    loop(
        0, chunks, lambda chunk: sent_all(plane_in.at[1:xys, owners(chunk)], plane_send.at[chunk], plane_recv.at[chunk])
    )
    sent_all(z_in.at[1:zs], z_send, z_recv)
    sent_all(coeffs_ref.at[1:qs], coeff_send, coeff_recv)
    wait_all(part_ref.at[1:qs], part_send, part_recv)
    expected_ref[...] = jnp.sum(part_ref[...], axis=0) / gram_all[0, rows : rows + 1, 0:1]
    sent_all(part_ref.at[1:qs], part_send, part_recv)


def exposure_kernel(coeffs_ref, start_ref, shocks_ref, thresholds_ref, exposure_ref):
    dates, sets, _ = exposure_ref.shape
    width = 2 * start_ref.shape[0]
    high, low = split(coeffs_ref[...].reshape(sets, LANES))
    coeffs = jnp.concatenate([high, low, high], axis=1)
    limits = jnp.broadcast_to(0.25 * thresholds_ref[...].astype(F32), (LANES, sets)).T
    state = start_ref[...]
    for date in range(dates):
        high, low = split(make_basis(state))
        zero = jnp.zeros_like(high)
        parts = [entries if k == date else zero for entries in (high, high, low) for k in range(dates)]
        exposure_ref[date] = jnp.maximum(dot(coeffs, jnp.concatenate(parts, axis=0), 1, 0) - limits[:, 0:1], 0.0)
        state = 0.8 * state + 0.6 * shocks_ref[date]


def body(
    start_state, shocks, loadings, strikes, notionals, trade_set, live_counts, weights, thresholds
):
    zs, qs = lax.axis_size("trade"), lax.axis_size("path")
    xys = qs // 2
    paths, factors = start_state.shape
    dates = shocks.shape[0]
    width = 2 * factors
    slots = loadings.shape[1] // 2
    size = min(1024, slots)
    sets = thresholds.shape[0]
    per = sets // qs
    chunks = zs
    tall = (width // qs + 8) // 8 * 8
    vmem = pl.BlockSpec(memory_space=pltpu.VMEM)
    hbm = pl.BlockSpec(memory_space=pl.ANY)
    dma = pltpu.SemaphoreType.DMA
    coeffs, expected = pl.pallas_call(
        functools.partial(kernel, zs, xys, size),
        out_shape=(
            jax.ShapeDtypeStruct((qs, per, LANES), F32),
            jax.ShapeDtypeStruct((dates, sets), F32),
        ),
        in_specs=[hbm] * 4 + [pl.BlockSpec(memory_space=pltpu.SMEM)] + [hbm] * 4,
        out_specs=(vmem, vmem),
        scratch_shapes=[
            pltpu.VMEM((factors, paths), F32),
            pltpu.VMEM((dates, factors, paths), F32),
            pltpu.VMEM((1, paths), jnp.int32),
            pltpu.VMEM((1, sets), jnp.int32),
            pltpu.VMEM((factors, slots), F32),
            pltpu.VMEM((1, slots), F32),
            pltpu.VMEM((1, slots), F32),
            pltpu.VMEM((1, slots), jnp.int32),
            dma((8,)),
            pltpu.VMEM(((dates + 1) * factors + 8, paths), F32),
            pltpu.VMEM(((dates + 1) * factors + 8, paths), F32),
            pltpu.VMEM((2, dates, paths, 4 * factors), BF16),
            pltpu.VMEM((2, dates, 2 * width, paths), BF16),
            pltpu.VMEM((dates, 3 * dates * width, paths), BF16),
            pltpu.VMEM((LANES, slots), F32),
            pltpu.VMEM((2 * LANES, slots), BF16),
            pltpu.VMEM((qs, tall, LANES), F32),
            pltpu.VMEM((qs, tall, LANES), F32),
            pltpu.VMEM((tall, LANES), F32),
            pltpu.VMEM((qs, tall, LANES), F32),
            pltpu.VMEM((width, LANES), F32),
            pltpu.VMEM((zs, 2, xys, per, LANES), F32),
            pltpu.VMEM((zs, xys, per, LANES), F32),
            pltpu.VMEM((zs, xys, per, LANES), F32),
            pltpu.VMEM((xys, zs, per, LANES), F32),
            pltpu.VMEM((zs, per, LANES), F32),
            pltpu.VMEM((zs, per, LANES), F32),
            pltpu.VMEM((per, LANES), F32),
            pltpu.VMEM((qs, per, LANES), F32),
            pltpu.VMEM((qs, dates, sets), F32),
            dma, dma, dma, dma, dma, dma, dma((chunks,)), dma((chunks,)), dma((chunks,)), dma((chunks,)),
            dma, dma, dma, dma, dma, dma,
        ],
        compiler_params=pltpu.CompilerParams(
            collective_id=0, has_side_effects=True, vmem_limit_bytes=56 << 20
        ),
        name="exposures",
    )(
        start_state.T, shocks.transpose(0, 2, 1), weights.reshape(1, -1), thresholds.reshape(1, -1), live_counts,
        loadings, strikes.reshape(1, -1), notionals.reshape(1, -1), trade_set.reshape(1, -1),
    )
    exposure = pl.pallas_call(
        exposure_kernel,
        out_shape=jax.ShapeDtypeStruct((dates, sets, paths), F32),
        in_specs=[vmem] * 4,
        out_specs=vmem,
        compiler_params=pltpu.CompilerParams(vmem_limit_bytes=56 << 20),
        name="exposure",
    )(coeffs, start_state.T, shocks.transpose(0, 2, 1), thresholds.reshape(1, -1))
    return exposure, expected


def solution(mesh):
    placed = (
        P("path", None),
        P(None, "path", None),
        P(None, "trade"),
        P("trade"),
        P("trade"),
        P("trade"),
        P(),
        P("path"),
        P("trade"),
    )
    return jax.shard_map(
        body,
        mesh=mesh,
        in_specs=placed,
        out_specs=(P(None, "trade", "path"), P(None, "trade")),
        check_vma=False,
    )
```
